256 devices in a mesh: dp: 16 (over z, core), expert: 16 (over y, x).
Axes of the slice: x: 4, y: 4, z: 8, core: 2. Of those that a mesh axis runs over, the one named last changes fastest.
Arguments:
- ssm_state: bfloat16 [1024, 16, 4096], P('expert', None, 'dp'), may hold values from -6 to 6
- conv_state: bfloat16 [1024, 3, 4096], P('expert', None, 'dp'), may hold values from -6 to 6
- new_slot: int32 [1024], replicated, may hold values from 0 to 1023, as said below
- conv_input: bfloat16 [1024, 4096], P('expert', 'dp'), may hold values from -6 to 6
- gate_input: bfloat16 [1024, 4096], P('expert', 'dp'), may hold values from -6 to 6
- conv_weight: float32 [4, 4096], P(None, 'dp'), may hold values from -3 to 3
- conv_bias: float32 [4096], P('dp'), may hold values from -3 to 3
- x_proj_weight: bfloat16 [4096, 288], P('dp'), may hold values from -0.09375 to 0.09375
- step_weight: bfloat16 [256, 4096], P(None, 'dp'), may hold values from -0.375 to 0.375
- step_bias: float32 [4096], P('dp'), may hold values from -3 to -0.5
- decay_log: float32 [16, 4096], P(None, 'dp'), may hold values from 0 to 2
- skip_gain: float32 [4096], P('dp'), may hold values from 0.5 to 1.5
- out_proj_weight: bfloat16 [4096, 4096], P('dp', 'expert'), may hold values from -0.09375 to 0.09375
- residual: bfloat16 [1024, 4096], P(None, 'expert'), may hold values from -6 to 6
- norm_gain: float32 [4096], replicated, may hold values from 0.1 to 1.9
- routes: int32 [1024, 2], replicated, may hold values from 0 to 15, all different within a row; in each aligned block of 64 rows (0 to 63, 64 to 127, ...) at most 20 rows name the same one
- gate_weight: float32 [1024, 2], replicated, may hold values from 0.1 to 0.9
- expert_gate: bfloat16 [16, 4096, 7168], P('expert', None, 'dp'), may hold values from -0.09375 to 0.09375
- expert_up: bfloat16 [16, 4096, 7168], P('expert', None, 'dp'), may hold values from -0.09375 to 0.09375
- expert_down: bfloat16 [16, 7168, 4096], P('expert', 'dp'), may hold values from -0.0625 to 0.0625
Outputs:
- ssm_new: bfloat16 [1024, 16, 4096], P('expert', None, 'dp')
- conv_new: bfloat16 [1024, 3, 4096], P('expert', None, 'dp')
- layer_out: bfloat16 [1024, 4096], P(None, 'expert')
The draws below stay inside these ranges and needn't reach their ends.
Inputs may be any that keep to these rules, and one draw needn't show every extreme that they name: new_slot is a permutation of the 1024 slots; slot s belongs to expert index s // 64. Of the 64 old slots of one expert index, at most 8 get new slots of any one expert index, and exactly 8 those of some expert index; every expert index sends the same multiset of such counts. `routes`: each row names 2 different experts; within each aligned block of 64 rows (the rows of one expert index) no expert is named by more than 20 rows, a bound that some block reaches.
All inputs are finite; a program needn't handle non-finite values.
Results may differ from the reference program's by a relative error of at most 0.012.
Values may be sent and summed in bfloat16 or wider, within the bound.
A program may use at most 128 MiB of HBM per device.

```python
import math
import jax
import jax.numpy as jnp
import numpy as np
from jax import lax

D = 4096
RK = 256
NS = 16
KC = 4
TOPK = 2
DI = 4096
FF = 7168
REQ_DEV = 64
REQ = 1024
EXPERTS = 16
CAP = 20


def draw_new_slot(key, part):
    row_count = REQ_DEV
    owners = REQ // REQ_DEV
    base = row_count // owners
    keys = jax.random.split(key, 6)
    pairing = jax.random.permutation(keys[0], owners)
    amplitude = jax.random.randint(keys[1], (owners // 2,), 0, base + 1).astype(jnp.int32)
    amplitude = amplitude.at[0].set(base)
    weights = jnp.zeros((owners,), jnp.int32)
    weights = weights.at[pairing[0::2]].set(base + amplitude)
    weights = weights.at[pairing[1::2]].set(base - amplitude)
    source_perm = jax.random.permutation(keys[2], owners)
    target_perm = jax.random.permutation(keys[3], owners)
    counts = weights[(target_perm[None, :] - source_perm[:, None]) % owners]
    ends = jnp.cumsum(counts, axis=1)
    starts = ends - counts
    places = jnp.arange(row_count, dtype=jnp.int32)
    target = jnp.sum((places[None, :, None] >= ends[:, None, :]).astype(jnp.int32), axis=2)
    within = places[None, :] - jnp.take_along_axis(starts, target, axis=1)
    offsets = jnp.cumsum(counts, axis=0) - counts
    position = jnp.take_along_axis(offsets, target, axis=1) + within
    shuffles = jax.vmap(lambda sub: jax.random.permutation(sub, row_count))(jax.random.split(keys[4], owners))
    new_place = shuffles[target, position]
    slot_sorted = target * row_count + new_place
    row_perm = jax.vmap(lambda sub: jax.random.permutation(sub, row_count))(jax.random.split(keys[5], owners))
    result = jnp.zeros((owners, row_count), jnp.int32)
    result = result.at[jnp.arange(owners)[:, None], row_perm].set(slot_sorted.astype(jnp.int32))
    return result.reshape(REQ)


def shard_levels(rng, shape, cuts, low, largest):
    factor_of = 1.0
    for axis_at, blocks in cuts:
        draws = jax.random.uniform(jax.random.fold_in(jax.random.fold_in(rng, 6), axis_at), (blocks,), jnp.float32, low / len(cuts), largest / len(cuts))
        factor_of = factor_of * jnp.repeat(jnp.exp(draws), shape[axis_at] // blocks).reshape((-1,) + (1,) * (len(shape) - 1 - axis_at))
    return factor_of


def routed_block(own_key, own, number, rows, number_of, top, most, skew):
    order = jax.random.permutation(own_key, number_of)
    heavy_load, ordinary = shares(number_of, rows * top, most, skew, True), shares(number_of, rows * top, most, skew, False)
    places = jnp.arange(number_of)

    def named(sizes, turn):
        used = int((sizes > 0).sum())
        fixed = max(1, used // 4)
        passed = fixed + (places - fixed + turn * (used - fixed)) % max(1, number_of - fixed)
        return jnp.zeros((number_of,), jnp.int32).at[order[jnp.where(places < fixed, places, passed)]].set(jnp.asarray(sizes, jnp.int32))

    sizes = jnp.where(number % 4 == 0, named(heavy_load, number // 4), named(ordinary, number - number // 4 - 1))
    mixed = jax.random.permutation(jax.random.fold_in(own, 3), number_of)
    giver, sink = mixed[0:number_of // 2 * 2:2], mixed[1:number_of // 2 * 2:2]
    slack = jnp.minimum(sizes[giver] - 1, most - sizes[sink]) // 2
    slack = jnp.where((giver == order[0]) | (sink == order[0]) | (sizes[sink] == 0), 0, jnp.maximum(slack, 0))
    passed = jax.random.randint(jax.random.fold_in(own, 4), (number_of // 2,), 0, 1 << 20) % (slack + 1)
    sizes = sizes.at[giver].add(-passed).at[sink].add(passed)
    members = jnp.searchsorted(jnp.cumsum(sizes), jnp.arange(rows * top), side="right").astype(jnp.int32)
    grid = members.reshape(top, rows).T
    grid = grid[jax.random.permutation(jax.random.fold_in(own, 1), rows)]
    turn = jax.random.randint(jax.random.fold_in(own, 2), (rows, 1), 0, top)
    return jnp.take_along_axis(grid, (jnp.arange(top)[None, :] + turn) % top, axis=1)


def shares(amount, total, bound, skew, full):
    portions = [(1 << 20) // math.isqrt(grade ** skew) + 1 for grade in range(1, amount + 1)]
    largest = bound if full else min(bound, max(-(-total // amount), total * portions[0] // sum(portions)))
    least = 1 if total - largest >= amount - 1 else 0
    holding, rest = [largest] + [least] * (amount - 1), total - largest - least * (amount - 1)
    while rest > 0:
        movable = [i for i in range(1, amount) if holding[i] < largest] or [i for i in range(1, amount) if holding[i] < bound]
        whole, remaining = sum([portions[i] for i in movable]), rest
        for i in movable:
            more = min(bound - holding[i], max(1, remaining * portions[i] // whole), rest)
            holding[i] = holding[i] + more
            rest = rest - more
    return np.array(holding)


def scatter_about(key, extent, deviation, most, cuts=(), kind=jnp.bfloat16):
    entries = deviation * jax.random.normal(key, extent, jnp.float32)
    if cuts:
        entries = entries * shard_levels(key, extent, cuts, -0.22, 0.18)
    return jnp.clip(entries, -most, most).astype(kind)


def setup_inputs(seed: int = 0) -> dict:
    key_list = jax.random.split(jax.random.key(seed), 21)
    ssm_state = scatter_about(key_list[0], (REQ, NS, DI), 1.0, 6.0, ((0, 16), (2, 16)))
    conv_state = scatter_about(key_list[1], (REQ, KC - 1, DI), 1.0, 6.0, ((0, 16), (2, 16)))
    new_slot = draw_new_slot(jax.random.fold_in(key_list[20], 71), 0)
    conv_input = scatter_about(key_list[3], (REQ, DI), 1.0, 6.0, ((0, 16), (1, 16)))
    gate_input = scatter_about(key_list[4], (REQ, DI), 1.0, 6.0, ((0, 16), (1, 16)))
    conv_weight = scatter_about(key_list[5], (KC, DI), KC ** -0.5, 3.0, ((1, 16),), jnp.float32)
    conv_bias = scatter_about(key_list[6], (DI,), 0.5, 3.0, ((0, 16),), jnp.float32)
    x_proj_weight = scatter_about(key_list[7], (DI, RK + 2 * NS), DI ** -0.5, 0.09375, ((0, 16),))
    step_weight = scatter_about(key_list[8], (RK, DI), RK ** -0.5, 0.375, ((1, 16),))
    step_bias = jnp.clip(-3.0 + 2.5 * jax.random.uniform(key_list[9], (DI,), jnp.float32) ** shard_levels(key_list[9], (DI,), ((0, 16),), -0.2, 0.2), -3.0, -0.5)
    decay_log = jnp.clip(2.0 * jax.random.uniform(key_list[10], (NS, DI), jnp.float32) ** shard_levels(key_list[10], (NS, DI), ((1, 16),), -0.2, 0.2), 0.0, 2.0)
    skip_gain = jnp.clip(0.5 + 1.0 * jax.random.uniform(key_list[11], (DI,), jnp.float32) ** shard_levels(key_list[11], (DI,), ((0, 16),), -0.2, 0.2), 0.5, 1.5)
    out_proj_weight = scatter_about(key_list[12], (DI, D), DI ** -0.5, 0.09375, ((0, 16), (1, 16)))
    residual = scatter_about(key_list[13], (REQ, D), 1.0, 6.0, ((1, 16),))
    norm_gain = jnp.clip(1.0 + 0.18 * jax.random.normal(key_list[14], (D,), jnp.float32), 0.1, 1.9)
    routes_keys = jax.random.split(jax.random.fold_in(key_list[15], 1), REQ // REQ_DEV)
    routes_turns = jax.random.permutation(jax.random.fold_in(key_list[15], 3), REQ // REQ_DEV)
    routes = jax.vmap(lambda own, number: routed_block(jax.random.fold_in(key_list[15], 2), own, number, REQ_DEV, EXPERTS, TOPK, CAP, 2))(routes_keys, routes_turns).reshape((REQ, TOPK))
    gate_weight = jnp.clip(jax.random.uniform(key_list[16], (REQ, TOPK), jnp.float32, 0.1, 0.9), 0.1, 0.9)
    expert_gate = scatter_about(key_list[17], (EXPERTS, D, FF), D ** -0.5, 0.09375, ((0, 16), (2, 16)))
    expert_up = scatter_about(key_list[18], (EXPERTS, D, FF), D ** -0.5, 0.09375, ((0, 16), (2, 16)))
    expert_down = scatter_about(key_list[19], (EXPERTS, FF, D), FF ** -0.5, 0.0625, ((0, 16), (1, 16)))
    return {"ssm_state": ssm_state, "conv_state": conv_state, "new_slot": new_slot, "conv_input": conv_input, "gate_input": gate_input, "conv_weight": conv_weight, "conv_bias": conv_bias, "x_proj_weight": x_proj_weight, "step_weight": step_weight, "step_bias": step_bias, "decay_log": decay_log, "skip_gain": skip_gain, "out_proj_weight": out_proj_weight, "residual": residual, "norm_gain": norm_gain, "routes": routes, "gate_weight": gate_weight, "expert_gate": expert_gate, "expert_up": expert_up, "expert_down": expert_down}


def reference(ssm_state, conv_state, new_slot, conv_input, gate_input, conv_weight, conv_bias, x_proj_weight, step_weight, step_bias, decay_log, skip_gain, out_proj_weight, residual, norm_gain, routes, gate_weight, expert_gate, expert_up, expert_down):
    moved_ssm = jnp.zeros_like(ssm_state).at[new_slot].set(ssm_state)
    moved_conv = jnp.zeros_like(conv_state).at[new_slot].set(conv_state)
    window = jnp.concatenate([moved_conv, conv_input[:, None, :]], axis=1)
    conv_new = window[:, 1:, :]
    conv_sum = lax.optimization_barrier(jnp.sum(window.astype(jnp.float32) * conv_weight[None, :, :], axis=1)) + conv_bias[None, :]
    activated = jax.nn.silu(conv_sum).astype(jnp.bfloat16)
    projected = jnp.dot(activated, x_proj_weight, preferred_element_type=jnp.float32)
    step_low = projected[:, :RK]
    b_coef = projected[:, RK:RK + NS]
    c_coef = projected[:, RK + NS:]
    step_norm = (step_low * lax.rsqrt(lax.optimization_barrier(jnp.mean(step_low * step_low, axis=1, keepdims=True)) + 1e-06)).astype(jnp.bfloat16)
    step_size = jax.nn.softplus(jnp.dot(step_norm, step_weight, preferred_element_type=jnp.float32) + step_bias[None, :])
    act_float = activated.astype(jnp.float32)
    decays = jnp.exp(step_size[:, None, :] * (-jnp.exp(decay_log))[None, :, :])
    states = decays * moved_ssm.astype(jnp.float32) + (step_size * act_float)[:, None, :] * b_coef[:, :, None]
    ssm_new = states.astype(jnp.bfloat16)
    gated_out = ((lax.optimization_barrier(jnp.sum(c_coef[:, :, None] * states, axis=1)) + skip_gain[None, :] * act_float) * jax.nn.silu(gate_input.astype(jnp.float32))).astype(jnp.bfloat16)
    stream = (residual.astype(jnp.float32) + jnp.dot(gated_out, out_proj_weight, preferred_element_type=jnp.float32)).astype(jnp.bfloat16)
    stream_f = stream.astype(jnp.float32)
    normed = (stream_f * lax.rsqrt(lax.optimization_barrier(jnp.mean(stream_f * stream_f, axis=1, keepdims=True)) + 1e-05) * norm_gain[None, :]).astype(jnp.bfloat16)
    limit = REQ // REQ_DEV * CAP

    def one_expert(expert_id):
        chosen = routes == expert_id
        row_weight = lax.optimization_barrier(jnp.sum(jnp.where(chosen, gate_weight, jnp.zeros_like(gate_weight)), axis=1))
        used = jnp.any(chosen, axis=1)
        keys = jnp.where(used, 0, 1).astype(jnp.int32)
        picked = jnp.argsort(keys, stable=True)[:limit].astype(jnp.int32)
        rows_in = normed[picked]
        gate_val = jnp.dot(rows_in, expert_gate[expert_id], preferred_element_type=jnp.float32)
        up_val = jnp.dot(rows_in, expert_up[expert_id], preferred_element_type=jnp.float32)
        hidden = (jax.nn.silu(gate_val) * up_val).astype(jnp.bfloat16)
        result = jnp.dot(hidden, expert_down[expert_id], preferred_element_type=jnp.float32)
        return (picked, result * row_weight[picked][:, None])
    picked_all, contrib = lax.map(one_expert, jnp.arange(EXPERTS, dtype=jnp.int32))
    expert_mix = jnp.zeros((REQ, D), jnp.float32).at[picked_all.reshape(-1)].add(contrib.reshape(-1, D))
    layer_out = (stream_f + expert_mix).astype(jnp.bfloat16)
    return (ssm_new, conv_new, layer_out)
```

```python
import functools

import jax
import jax.numpy as jnp
from jax import lax
from jax.experimental import pallas as pl
from jax.experimental.pallas import tpu as pltpu
from jax.sharding import PartitionSpec as P

MESH = pl.DeviceIdType.MESH
F32 = jnp.float32
BF16 = jnp.bfloat16
LANES = 128


def iota(shape, axis):
    return lax.broadcasted_iota(jnp.int32, shape, axis)


def ones_where(mask):
    return jnp.where(mask, 1.0, 0.0)


def dot(a, b):
    return jnp.dot(a, b, preferred_element_type=F32)


def dot_t(a, b):
    return lax.dot_general(a, b, (((1,), (1,)), ((), ())), preferred_element_type=F32)


def silu(v):
    return v / (1.0 + jnp.exp(-v))


def times(lo, hi, step):
    def run(i, carry):
        step(i)
        return carry

    lax.fori_loop(lo, hi, run, 0)


def kernel(
    dims,
    ssm_hbm, conv_ref, slot_ref, cin_ref, gin_ref, cw_ref, cb_ref, xp_ref, sw_ref, sb_ref,
    dl_ref, sg_ref, wo_ref, res_hbm, ng_ref, rt_ref, gw_ref, wg_hbm, wu_hbm, wd_hbm,
    ssm_out, conv_out, layer_out,
    ssm_v, ssm_f, res_v, wg_v, wu_v, wd_v,
    conv_s, conv_r, ssm_s, ssm_r, ssm_o, conv_o,
    proj_s, proj_r, proj_c, proj_g,
    gat, mix_s, mix_b, mix_t, mix_r, stream_v,
    disp_s, xb, xn, acc_g, acc_u, hid, yp, ysib, yrs, yrr, yls, ylr,
    ret_s, ret_r, dhi_v, dlo_v, outg,
    load_sem, cs_sem, cr_sem, ss_sem, sr_sem, store_sem,
    ps_sem, pr_sem, qs_sem, qr_sem, gs_sem, gr_sem,
    ms_sem, mr_sem, bs_sem, br_sem, ds_sem, dr_sem,
    xrs, xrr, xls, xlr, xss, xsr,
    yss_sem, ysr_sem, yrs_sem, yrr_sem, yls_sem, ylr_sem,
    rs_sem, rr_sem, os_sem, or_sem, ts_sem, tr_sem,
):
    NE, NZ, ROWS, MC, CAP = dims
    ND = 2 * NZ
    PC = 2 * CAP
    LW = 2 * ROWS
    NS = dl_ref.shape[0]
    WB = cin_ref.shape[1]
    RK = sw_ref.shape[0]
    D = NE * WB
    HE = NE // 2
    MP = xn.shape[1]
    shift = ROWS.bit_length() - 1
    d = lax.axis_index("dp")
    e = lax.axis_index("expert")
    z = d // 2
    c = d % 2

    def remote(src, dst, ssem, rsem, dev):
        return pltpu.make_async_remote_copy(
            src_ref=src, dst_ref=dst, send_sem=ssem, recv_sem=rsem, device_id=dev, device_id_type=MESH
        )

    barrier = pltpu.get_barrier_semaphore()
    times(1, NE, lambda i: pl.semaphore_signal(barrier, inc=1, device_id=(d, (e + i) % NE), device_id_type=MESH))
    times(1, ND, lambda i: pl.semaphore_signal(barrier, inc=1, device_id=((d + i) % ND, e), device_id_type=MESH))

    row0 = pl.multiple_of(z * LW, LW)
    lane0 = pl.multiple_of(c * LANES, LANES)
    loads = [
        pltpu.make_async_copy(ssm_hbm, ssm_v, load_sem.at[0]),
        pltpu.make_async_copy(res_hbm.at[pl.ds(row0, LW), pl.ds(lane0, LANES)], res_v, load_sem.at[1]),
        pltpu.make_async_copy(wg_hbm, wg_v, load_sem.at[2]),
        pltpu.make_async_copy(wu_hbm, wu_v, load_sem.at[3]),
        pltpu.make_async_copy(wd_hbm, wd_v, load_sem.at[4]),
    ]
    for load in loads:
        load.start()

    mine = slot_ref[pl.ds(e // 2, 1), :]
    mine = jnp.where(e % 2 == 0, mine[:, :ROWS], mine[:, ROWS:])
    target = lax.shift_right_logical(mine, shift)
    target_hot = ones_where(iota((NE, ROWS), 0) == target)
    before = ones_where(iota((ROWS, ROWS), 0) < iota((ROWS, ROWS), 1)).astype(BF16)
    ahead = dot(target_hot.astype(BF16), before)
    earlier = jnp.sum(target_hot * ahead, axis=0, keepdims=True).astype(jnp.int32)
    pack = ones_where(iota((NE * MC, ROWS), 0) == target * MC + earlier).astype(BF16)
    for k in range(3):
        conv_s[:, k] = dot(pack, conv_ref[k]).reshape(NE, MC, WB).astype(BF16)

    pl.semaphore_wait(barrier, NE - 1 + ND - 1)

    def to_experts(src_of, dst, ssem, rsem):
        def one(i):
            p = (e + i) % NE
            remote(src_of(p), dst, ssem.at[i], rsem.at[e], (d, p)).start()

        times(1, NE, one)

    def sent_experts(src_of, dst, ssem, rsem):
        def one(i):
            p = (e + i) % NE
            remote(src_of(p), dst, ssem.at[i], rsem.at[e], (d, p)).wait_send()

        times(1, NE, one)

    def from_experts(dst_of, ssem, rsem):
        def one(i):
            p = (e + NE - i) % NE
            remote(dst_of(p), dst_of(p), ssem.at[i], rsem.at[p], (d, p)).wait_recv()

        times(1, NE, one)

    to_experts(lambda p: conv_s.at[p], conv_r.at[e], cs_sem, cr_sem)
    conv_r[e] = conv_s[e]

    loads[0].wait()
    ssm_f[...] = ssm_v[...].astype(F32)
    for n in range(NS):
        ssm_s[:, n] = dot(pack, ssm_f[:, n, :].astype(BF16)).reshape(NE, MC, WB).astype(BF16)
    to_experts(lambda p: ssm_s.at[p], ssm_r.at[e], ss_sem, sr_sem)
    ssm_r[e] = ssm_s[e]

    slots = slot_ref[...]
    arriving = ones_where(lax.shift_right_logical(slots, shift) == e)
    lane = iota((LW, LW), 1)
    sub = iota((LW, LW), 0)
    before2 = ones_where((sub < lane) & ((sub < ROWS) == (lane < ROWS))).astype(BF16)
    rank = dot(arriving.astype(BF16), before2)
    place = (slots & (ROWS - 1)).astype(F32) + 1.0
    half = iota((NZ, LW), 1) >= ROWS
    to_lane = iota((NZ, NE * MC), 1) - iota((NZ, NE * MC), 0) * (2 * MC)
    spread = jnp.zeros((NZ, NE * MC), F32)
    for h in range(2):
        live = (arriving > 0.0) & (half == bool(h))
        for k in range(MC):
            found = jnp.sum(jnp.where(live & (rank == float(k)), place, 0.0), axis=1, keepdims=True)
            spread = spread + jnp.where(to_lane == h * MC + k, found, 0.0)
    row_of = jnp.sum(spread, axis=0, keepdims=True).astype(jnp.int32) - 1
    unpack = ones_where(iota((ROWS, NE * MC), 0) == row_of).astype(BF16)

    from_experts(lambda p: conv_r.at[p], cs_sem, cr_sem)
    window = []
    for k in range(3):
        got = conv_r[:, k].astype(F32).reshape(NE * MC, WB).astype(BF16)
        window.append(dot(unpack, got))
    conv_o[0] = window[1].astype(BF16)
    conv_o[1] = window[2].astype(BF16)
    conv_o[2] = cin_ref[...]
    window.append(cin_ref[...].astype(F32))
    total = window[0] * cw_ref[0:1, :]
    for k in range(1, 4):
        total = total + window[k] * cw_ref[k : k + 1, :]
    activated = silu(total + cb_ref[...]).astype(BF16)
    act = activated.astype(F32)
    partial = dot_t(activated, xp_ref[...])
    RZ = ROWS // NZ
    proj_s[...] = jnp.zeros_like(proj_s)
    proj_s[:, :, : RK + 2 * NS] = partial.reshape(NZ, RZ, RK + 2 * NS)

    def proj_src(p):
        return proj_s.at[p // 2, :, pl.ds(pl.multiple_of((p % 2) * LANES, LANES), RK)]

    def to_dp(src_of, dst, ssem, rsem):
        def one(i):
            p = (d + i) % ND
            remote(src_of(p), dst, ssem.at[i], rsem.at[d], (p, e)).start()

        times(1, ND, one)

    def sent_dp(src_of, dst, ssem, rsem):
        def one(i):
            p = (d + i) % ND
            remote(src_of(p), dst, ssem.at[i], rsem.at[d], (p, e)).wait_send()

        times(1, ND, one)

    def from_dp(dst_of, ssem, rsem):
        def one(i):
            p = (d + ND - i) % ND
            remote(dst_of(p), dst_of(p), ssem.at[i], rsem.at[p], (p, e)).wait_recv()

        times(1, ND, one)

    to_dp(proj_src, proj_r.at[d], ps_sem, pr_sem)
    proj_r[d] = proj_s[z, :, pl.ds(lane0, RK)]
    store_conv = pltpu.make_async_copy(conv_o, conv_out, store_sem.at[0])
    store_conv.start()

    r0 = rt_ref[0:1, pl.ds(row0, LW)]
    r1 = rt_ref[1:2, pl.ds(row0, LW)]
    g0 = gw_ref[0:1, pl.ds(row0, LW)]
    g1 = gw_ref[1:2, pl.ds(row0, LW)]
    expert_id = iota((NE, LW), 0)
    named = ones_where((expert_id == r0) | (expert_id == r1))
    weight = jnp.where(expert_id == r0, g0, 0.0) + jnp.where(expert_id == r1, g1, 0.0)
    w_hi = weight.astype(BF16).astype(F32)
    w_lo = weight - w_hi
    in_block = dot(named.astype(BF16), before2).astype(jnp.int32)
    seat = in_block + jnp.where(iota((NE, LW), 1) >= ROWS, CAP, 0)
    seat = jnp.where(named > 0.0, seat, -1)
    seat_id = iota((PC, LW), 0)
    rows_d, rows_hi, rows_lo = [], [], []
    for k in range(NE):
        hit = seat_id == seat[k : k + 1, :]
        rows_d.append(jnp.where(hit, 1.0, 0.0))
        rows_hi.append(jnp.where(hit, w_hi[k : k + 1, :], 0.0))
        rows_lo.append(jnp.where(hit, w_lo[k : k + 1, :], 0.0))
    dispatch = jnp.concatenate(rows_d, axis=0).astype(BF16)
    dhi_v[...] = jnp.concatenate(rows_hi, axis=0).T.astype(BF16)
    dlo_v[...] = jnp.concatenate(rows_lo, axis=0).T.astype(BF16)

    from_dp(lambda p: proj_r.at[p], ps_sem, pr_sem)
    summed = proj_r[0]
    for k in range(1, ND):
        summed = summed + proj_r[k]
    proj_c[...] = summed
    to_dp(lambda p: proj_c, proj_g.at[c, z], qs_sem, qr_sem)
    proj_g[c, z] = summed
    from_dp(lambda p: proj_g.at[p % 2, p // 2], qs_sem, qr_sem)
    step_low = proj_g[0].reshape(ROWS, RK)
    coef = proj_g[1][:, :, RK - LANES :].reshape(ROWS, LANES)
    mean = jnp.sum(step_low * step_low, axis=1, keepdims=True) * (1.0 / RK)
    step_norm = (step_low * lax.rsqrt(mean + 1e-06)).astype(BF16)
    pre = dot(step_norm, sw_ref[...]) + sb_ref[...]
    step = jnp.maximum(pre, 0.0) + jnp.log1p(jnp.exp(-jnp.abs(pre)))
    decay = -jnp.exp(dl_ref[...])
    push = step * act

    from_experts(lambda p: ssm_r.at[p], ss_sem, sr_sem)
    y = sg_ref[...] * act
    read = jnp.zeros_like(y)
    for n in range(NS):
        got = ssm_r[:, n].astype(F32).reshape(NE * MC, WB).astype(BF16)
        moved = dot(unpack, got)
        state = jnp.exp(step * decay[n : n + 1, :]) * moved + push * coef[:, n : n + 1]
        ssm_f[:, n, :] = state
        read = read + coef[:, NS + n : NS + n + 1] * state
    gate = gin_ref[...].astype(F32)
    gated = ((read + y) * silu(gate)).astype(BF16)
    gat[e] = gated
    to_experts(lambda p: gat.at[e], gat.at[e], gs_sem, gr_sem)
    ssm_o[...] = ssm_f[...].astype(BF16)
    store_ssm = pltpu.make_async_copy(ssm_o, ssm_out, store_sem.at[1])
    store_ssm.start()

    from_experts(lambda p: gat.at[p], gs_sem, gr_sem)
    for k in range(NZ):
        mixed = dot(gat[2 * k : 2 * k + 2].reshape(LW, WB), wo_ref[...])
        mix_s[0, k] = mixed[:, :LANES].astype(BF16)
        mix_s[1, k] = mixed[:, LANES:].astype(BF16)
    sibling = (2 * z + 1 - c, e)
    mix_swap = remote(mix_s.at[1 - c], mix_b, bs_sem.at[0], br_sem.at[0], sibling)
    mix_swap.start()
    mix_swap.wait_recv()
    for k in range(NZ):
        mix_t[k] = (mix_s[c, k].astype(F32) + mix_b[k].astype(F32)).astype(BF16)

    def send_mix(i):
        p = (z + i) % NZ
        return remote(mix_t.at[p], mix_r.at[z], ms_sem.at[i], mr_sem.at[z], (2 * p + c, e))

    times(1, NZ, lambda i: send_mix(i).start())
    mix_r[z] = mix_t[z]

    def recv_mix(i):
        p = (z + NZ - i) % NZ
        remote(mix_r.at[p], mix_r.at[p], ms_sem.at[i], mr_sem.at[p], (2 * p + c, e)).wait_recv()

    times(1, NZ, recv_mix)
    loads[1].wait()
    mixed = mix_r[0].astype(F32)
    for k in range(1, NZ):
        mixed = mixed + mix_r[k].astype(F32)
    stream = (res_v[...].astype(F32) + mixed).astype(BF16)
    stream_v[...] = stream

    disp_s[...] = dot(dispatch, stream).reshape(NE, PC, LANES).astype(BF16)
    to_experts(lambda p: disp_s.at[p], xb.at[c, z, e], ds_sem, dr_sem)
    xb[c, z, e] = disp_s[e]
    from_experts(lambda p: xb.at[c, z, p], ds_sem, dr_sem)

    right = (2 * ((z + 1) % NZ) + c, e)
    left = (2 * ((z + NZ - 1) % NZ) + c, e)
    far = NZ // 2
    hops_r = (far, NZ - 1 - far)
    hops_l = (NZ - 1 - far, far)
    halves = (pl.ds(0, HE), pl.ds(HE, HE))

    def back(s):
        return (z + NZ - s) % NZ

    def ahead_z(s):
        return (z + s) % NZ

    def ring_right(h, s):
        p = back(s)
        part = xb.at[c, p, halves[h]]
        return remote(part, part, xrs.at[h, s], xrr.at[h, s], right)

    def ring_left(h, s):
        p = ahead_z(s)
        part = xb.at[c, p, halves[h]]
        return remote(part, part, xls.at[h, s], xlr.at[h, s], left)

    def wait_right(h, s):
        part = xb.at[c, back(s + 1), halves[h]]
        remote(part, part, xrs.at[h, s], xrr.at[h, s], right).wait_recv()

    def wait_left(h, s):
        part = xb.at[c, ahead_z(s + 1), halves[h]]
        remote(part, part, xls.at[h, s], xlr.at[h, s], left).wait_recv()

    def over(h, p):
        part = xb.at[c, p, halves[h]]
        return remote(part, part, xss.at[h, p], xsr.at[h, p], sibling)

    def wait_over(h, p):
        part = xb.at[1 - c, p, halves[h]]
        remote(part, part, xss.at[h, p], xsr.at[h, p], sibling).wait_recv()

    def normalise(p):
        square = jnp.zeros((PC, LANES), F32)
        for k in range(NE):
            for m in range(2):
                v = xb[m, p, k].astype(F32)
                square = square + v * v
        scale = lax.rsqrt(jnp.sum(square, axis=1, keepdims=True) * (1.0 / D) + 1e-05)
        for k in range(NE):
            for m in range(2):
                v = xb[m, p, k].astype(F32) * scale * ng_ref[2 * k + m : 2 * k + m + 1, :]
                if MP > PC:
                    v = jnp.concatenate([v, jnp.zeros((MP - PC, LANES), F32)], axis=0)
                xn[p, :, (2 * k + m) * LANES : (2 * k + m + 1) * LANES] = v.astype(BF16)

    for s in range(far):
        for h in range(2):
            if 0 < s <= hops_r[h]:
                wait_right(h, s - 1)
            if s < hops_r[h]:
                ring_right(h, s).start()
            if 0 < s <= hops_l[h]:
                wait_left(h, s - 1)
            if s < hops_l[h]:
                ring_left(h, s).start()
        for p in [z] if s == 0 else [back(s), ahead_z(s)]:
            for h in range(2):
                over(h, p).start()
            for h in range(2):
                wait_over(h, p)
            normalise(p)
    last = ahead_z(far)
    for h in range(2):
        if hops_r[h] == far:
            wait_right(h, far - 1)
        if hops_l[h] == far:
            wait_left(h, far - 1)
        over(h, last).start()
    for h in range(2):
        wait_over(h, last)
    normalise(last)

    loads[2].wait()
    loads[3].wait()
    KC = min(D, 1024)
    acc_g[...] = jnp.zeros_like(acc_g)
    acc_u[...] = jnp.zeros_like(acc_u)

    def depth(k):
        at = pl.ds(pl.multiple_of(k * KC, KC), KC)
        x = xn[:, :, at].reshape(NZ * MP, KC)
        acc_g[...] += dot_t(x, wg_v[:, at])
        acc_u[...] += dot_t(x, wu_v[:, at])

    times(0, D // KC, depth)
    hid[...] = (silu(acc_g[...]) * acc_u[...]).astype(BF16)
    loads[4].wait()

    def down(h, k):
        at = pl.ds(pl.multiple_of((h * HE + k) * WB, WB), WB)
        out = dot(hid[...], wd_v[:, at]).reshape(NZ, MP, WB)[:, :PC].astype(BF16)
        yp[0, h, :, k] = out[:, :, :LANES]
        yp[1, h, :, k] = out[:, :, LANES:]

    def swap_y(h):
        return remote(yp.at[1 - c, h], ysib.at[h], yss_sem.at[h], ysr_sem.at[h], sibling)

    for h in range(2):
        times(0, HE, lambda k: down(h, k))
        swap_y(h).start()

    def own(h, p):
        return yp[c, h, p].astype(F32) + ysib[h, p].astype(F32)

    def chain_right(h, s):
        return remote(yrs.at[h, s], yrr.at[h, s], yrs_sem.at[h, s], yrr_sem.at[h, s], right)

    def chain_left(h, s):
        return remote(yls.at[h, s], ylr.at[h, s], yls_sem.at[h, s], ylr_sem.at[h, s], left)

    for s in range(far):
        for h in range(2):
            if s == 0:
                swap_y(h).wait_recv()
            if s < hops_r[h]:
                part = own(h, ahead_z(hops_r[h] - s))
                if s > 0:
                    chain_right(h, s - 1).wait_recv()
                    part = part + yrr[h, s - 1].astype(F32)
                yrs[h, s] = part.astype(BF16)
                chain_right(h, s).start()
            if s < hops_l[h]:
                part = own(h, back(hops_l[h] - s))
                if s > 0:
                    chain_left(h, s - 1).wait_recv()
                    part = part + ylr[h, s - 1].astype(F32)
                yls[h, s] = part.astype(BF16)
                chain_left(h, s).start()
    for h in range(2):
        part = own(h, z)
        if hops_r[h] > 0:
            chain_right(h, hops_r[h] - 1).wait_recv()
            part = part + yrr[h, hops_r[h] - 1].astype(F32)
        if hops_l[h] > 0:
            chain_left(h, hops_l[h] - 1).wait_recv()
            part = part + ylr[h, hops_l[h] - 1].astype(F32)
        ret_s[h * HE : (h + 1) * HE] = part.astype(BF16)

    to_experts(lambda p: ret_s.at[p], ret_r.at[e], rs_sem, rr_sem)
    ret_r[e] = ret_s[e]
    from_experts(lambda p: ret_r.at[p], rs_sem, rr_sem)
    back_rows = ret_r[...].astype(F32).reshape(NE * PC, LANES).astype(BF16)
    final = stream_v[...].astype(F32) + dot(dhi_v[...], back_rows) + dot(dlo_v[...], back_rows)
    outg[c, z] = final.astype(BF16)

    def send_out(i):
        p = (z + i) % NZ
        return remote(outg.at[c, z], outg.at[c, z], os_sem.at[i], or_sem.at[z], (2 * p + c, e))

    def wait_out(i):
        p = (z + NZ - i) % NZ
        remote(outg.at[c, p], outg.at[c, p], os_sem.at[i], or_sem.at[p], (2 * p + c, e)).wait_recv()

    def pass_out(p):
        return remote(outg.at[c, p], outg.at[c, p], ts_sem.at[p], tr_sem.at[p], sibling)

    times(1, NZ, lambda i: send_out(i).start())
    pass_out(z).start()

    def relay(i):
        wait_out(i)
        pass_out((z + NZ - i) % NZ).start()

    times(1, NZ, relay)

    def wait_pass(p):
        remote(outg.at[1 - c, p], outg.at[1 - c, p], ts_sem.at[p], tr_sem.at[p], sibling).wait_recv()

    times(0, NZ, wait_pass)
    for k in range(NZ):
        for m in range(2):
            layer_out[k * LW : (k + 1) * LW, m * LANES : (m + 1) * LANES] = outg[m, k]

    store_conv.wait()
    store_ssm.wait()
    sent_experts(lambda p: conv_s.at[p], conv_r.at[e], cs_sem, cr_sem)
    sent_experts(lambda p: ssm_s.at[p], ssm_r.at[e], ss_sem, sr_sem)
    sent_dp(proj_src, proj_r.at[d], ps_sem, pr_sem)
    sent_dp(lambda p: proj_c, proj_g.at[c, z], qs_sem, qr_sem)
    sent_experts(lambda p: gat.at[e], gat.at[e], gs_sem, gr_sem)
    mix_swap.wait_send()
    times(1, NZ, lambda i: send_mix(i).wait_send())
    sent_experts(lambda p: disp_s.at[p], xb.at[c, z, e], ds_sem, dr_sem)
    for h in range(2):
        for s in range(hops_r[h]):
            ring_right(h, s).wait_send()
            chain_right(h, s).wait_send()
        for s in range(hops_l[h]):
            ring_left(h, s).wait_send()
            chain_left(h, s).wait_send()
        swap_y(h).wait_send()
        times(0, NZ, lambda p: over(h, p).wait_send())
    sent_experts(lambda p: ret_s.at[p], ret_r.at[e], rs_sem, rr_sem)
    times(1, NZ, lambda i: send_out(i).wait_send())
    times(0, NZ, lambda p: pass_out(p).wait_send())


def body(
    ssm_state, conv_state, new_slot, conv_input, gate_input, conv_weight, conv_bias, x_proj_weight,
    step_weight, step_bias, decay_log, skip_gain, out_proj_weight, residual, norm_gain, routes,
    gate_weight, expert_gate, expert_up, expert_down,
):
    ROWS, NS, WB = ssm_state.shape
    NE = lax.axis_size("expert")
    NZ = lax.axis_size("dp") // 2
    RK = step_weight.shape[0]
    FB = expert_gate.shape[2]
    MC = 2 * ROWS // NE
    CAP = min(ROWS, 5 * ROWS * routes.shape[1] // (2 * NE))
    PC, LW, D, HE = 2 * CAP, 2 * ROWS, NE * WB, NE // 2
    MP = (PC + 15) // 16 * 16
    RZ = ROWS // NZ
    far = NZ // 2
    hbm = pl.BlockSpec(memory_space=pl.ANY)
    vmem = pl.BlockSpec(memory_space=pltpu.VMEM)
    V, S = pltpu.VMEM, pltpu.SemaphoreType.DMA
    scratch = [
        V((ROWS, NS, WB), BF16), V((ROWS, NS, WB), F32), V((LW, LANES), BF16),
        V((FB, D), BF16), V((FB, D), BF16), V((FB, D), BF16),
        V((NE, 3, MC, WB), BF16), V((NE, 3, MC, WB), BF16),
        V((NE, NS, MC, WB), BF16), V((NE, NS, MC, WB), BF16),
        V((ROWS, NS, WB), BF16), V((3, ROWS, WB), BF16),
        V((NZ, RZ, RK + LANES), F32), V((2 * NZ, RZ, RK), F32), V((RZ, RK), F32), V((2, NZ, RZ, RK), F32),
        V((NE, ROWS, WB), BF16), V((2, NZ, LW, LANES), BF16), V((NZ, LW, LANES), BF16),
        V((NZ, LW, LANES), BF16), V((NZ, LW, LANES), BF16), V((LW, LANES), BF16),
        V((NE, PC, LANES), BF16), V((2, NZ, NE, PC, LANES), BF16), V((NZ, MP, D), BF16),
        V((NZ * MP, FB), F32), V((NZ * MP, FB), F32), V((NZ * MP, FB), BF16),
        V((2, 2, NZ, HE, PC, LANES), BF16), V((2, NZ, HE, PC, LANES), BF16),
        V((2, far, HE, PC, LANES), BF16), V((2, far, HE, PC, LANES), BF16),
        V((2, far, HE, PC, LANES), BF16), V((2, far, HE, PC, LANES), BF16),
        V((NE, PC, LANES), BF16), V((NE, PC, LANES), BF16),
        V((LW, NE * PC), BF16), V((LW, NE * PC), BF16), V((2, NZ, LW, LANES), BF16),
        S((5,)), S((NE,)), S((NE,)), S((NE,)), S((NE,)), S((2,)),
        S((2 * NZ,)), S((2 * NZ,)), S((2 * NZ,)), S((2 * NZ,)), S((NE,)), S((NE,)),
        S((NZ,)), S((NZ,)), S((1,)), S((1,)), S((NE,)), S((NE,)),
        S((2, far)), S((2, far)), S((2, far)), S((2, far)), S((2, NZ)), S((2, NZ)),
        S((2,)), S((2,)), S((2, far)), S((2, far)), S((2, far)), S((2, far)),
        S((NE,)), S((NE,)), S((NZ,)), S((NZ,)), S((NZ,)), S((NZ,)),
    ]
    in_specs = [hbm] + [vmem] * 12 + [hbm] + [vmem] * 3 + [hbm] * 3
    call = pl.pallas_call(
        functools.partial(kernel, (NE, NZ, ROWS, MC, CAP)),
        out_shape=(
            jax.ShapeDtypeStruct((ROWS, NS, WB), BF16),
            jax.ShapeDtypeStruct((3, ROWS, WB), BF16),
            jax.ShapeDtypeStruct((NE * ROWS, WB), BF16),
        ),
        in_specs=in_specs,
        out_specs=(hbm, hbm, vmem),
        scratch_shapes=scratch,
        compiler_params=pltpu.CompilerParams(
            collective_id=0, has_side_effects=True, vmem_limit_bytes=56 * 1024 * 1024
        ),
        name="decode_step",
    )
    ssm_new, conv_new, layer = call(
        ssm_state, conv_state.transpose(1, 0, 2), new_slot.reshape(NZ, LW), conv_input, gate_input,
        conv_weight, conv_bias.reshape(1, WB), x_proj_weight.T, step_weight, step_bias.reshape(1, WB),
        decay_log, skip_gain.reshape(1, WB), out_proj_weight, residual, norm_gain.reshape(2 * NE, LANES),
        routes.T, gate_weight.T, expert_gate[0].T, expert_up[0].T, expert_down[0],
    )
    return ssm_new, conv_new.transpose(1, 0, 2), layer


def solution(mesh):
    in_specs = (
        P("expert", None, "dp"), P("expert", None, "dp"), P(), P("expert", "dp"), P("expert", "dp"),
        P(None, "dp"), P("dp"), P("dp", None), P(None, "dp"), P("dp"), P(None, "dp"), P("dp"),
        P("dp", "expert"), P(None, "expert"), P(), P(), P(),
        P("expert", None, "dp"), P("expert", None, "dp"), P("expert", "dp", None),
    )
    out_specs = (P("expert", None, "dp"), P("expert", None, "dp"), P(None, "expert"))
    return jax.shard_map(body, mesh=mesh, in_specs=in_specs, out_specs=out_specs, check_vma=False)
```

```python
import functools

import jax
import jax.numpy as jnp
from jax import lax
from jax.experimental import pallas as pl
from jax.experimental.pallas import tpu as pltpu
from jax.sharding import PartitionSpec as P

MESH = pl.DeviceIdType.MESH
F32 = jnp.float32
BF16 = jnp.bfloat16
LANES = 128


def iota(shape, axis):
    return lax.broadcasted_iota(jnp.int32, shape, axis)


def ones_where(mask):
    return jnp.where(mask, 1.0, 0.0)


def dot(a, b):
    return jnp.dot(a, b, preferred_element_type=F32)


def dot_t(a, b):
    return lax.dot_general(a, b, (((1,), (1,)), ((), ())), preferred_element_type=F32)


def silu(v):
    return v / (1.0 + jnp.exp(-v))


def times(lo, hi, step):
    def run(i, carry):
        step(i)
        return carry

    lax.fori_loop(lo, hi, run, 0)


def kernel(
    dims,
    ssm_hbm, conv_hbm, slot_hbm, cin_hbm, gin_hbm, cw_hbm, cb_hbm, xp_hbm, sw_hbm, sb_hbm,
    dl_hbm, sg_hbm, wo_hbm, res_hbm, ng_hbm, rt_hbm, gw_hbm, wg_hbm, wu_hbm, wd_hbm,
    ssm_out, conv_out, layer_out,
    conv_ref, slot_ref, cin_ref, gin_ref, cw_ref, cb_ref, xp_ref, sw_ref, sb_ref,
    dl_ref, sg_ref, wo_ref, ng_ref, rt_ref, gw_ref,
    ssm_v, ssm_f, moved_v, res_v, wg_v, wu_v, wd_v,
    conv_s, conv_r, ssm_s, ssm_r, ssm_o, conv_o,
    proj_s, proj_r, proj_c, proj_g,
    gat, mix_s, mix_b, mix_t, mix_r, stream_v,
    disp_s, xb, xn, acc_g, acc_u, hid, yp, ysib, yrs, yrr, yls, ylr,
    ret_s, ret_r, disp_v, dhi_v, dlo_v, outg,
    load_sem, cs_sem, cr_sem, ss_sem, sr_sem, store_sem,
    ps_sem, pr_sem, qs_sem, qr_sem, gs_sem, gr_sem,
    ms_sem, mr_sem, bs_sem, br_sem, ds_sem, dr_sem,
    xrs, xrr, xls, xlr, xss, xsr,
    yss_sem, ysr_sem, yrs_sem, yrr_sem, yls_sem, ylr_sem,
    rs_sem, rr_sem, os_sem, or_sem, ts_sem, tr_sem, out_sem,
):
    NE, NZ, ROWS, MC, CAP = dims
    ND = 2 * NZ
    PC = 2 * CAP
    LW = 2 * ROWS
    NS = dl_ref.shape[0]
    WB = cin_ref.shape[1]
    RK = sw_ref.shape[0]
    D = NE * WB
    NP = yrs.shape[0]
    HE = NE // NP
    MP = xn.shape[1]
    shift = ROWS.bit_length() - 1
    d = lax.axis_index("dp")
    e = lax.axis_index("expert")
    z = d // 2
    c = d % 2

    def remote(src, dst, ssem, rsem, dev):
        return pltpu.make_async_remote_copy(
            src_ref=src, dst_ref=dst, send_sem=ssem, recv_sem=rsem, device_id=dev, device_id_type=MESH
        )

    ending = []

    def go(copy):
        copy.start()
        ending.append(copy.wait_send)

    barrier = pltpu.get_barrier_semaphore()
    times(1, NE, lambda i: pl.semaphore_signal(barrier, inc=1, device_id=(d, (e + i) % NE), device_id_type=MESH))
    times(1, ND, lambda i: pl.semaphore_signal(barrier, inc=1, device_id=((d + i) % ND, e), device_id_type=MESH))

    row0 = pl.multiple_of(z * LW, LW)
    lane0 = pl.multiple_of(c * LANES, LANES)
    pair = pl.ds(row0, LW)
    sources = [
        (conv_hbm, conv_ref), (slot_hbm, slot_ref), (ssm_hbm, ssm_v), (rt_hbm.at[:, pair], rt_ref),
        (gw_hbm.at[:, pair], gw_ref), (cin_hbm, cin_ref), (cw_hbm, cw_ref), (cb_hbm, cb_ref), (xp_hbm, xp_ref),
        (sw_hbm, sw_ref), (sb_hbm, sb_ref), (dl_hbm, dl_ref), (sg_hbm, sg_ref), (gin_hbm, gin_ref), (wo_hbm, wo_ref),
        (res_hbm.at[pair, pl.ds(lane0, LANES)], res_v), (ng_hbm, ng_ref), (wg_hbm, wg_v), (wu_hbm, wu_v), (wd_hbm, wd_v),
    ]
    loads = [pltpu.make_async_copy(src, dst, load_sem.at[i]) for i, (src, dst) in enumerate(sources)]
    for load in loads:
        load.start()

    def loaded(lo, hi):
        for load in loads[lo:hi]:
            load.wait()

    loaded(0, 2)

    mine = slot_ref[pl.ds(e // 2, 1), :]
    mine = jnp.where(e % 2 == 0, mine[:, :ROWS], mine[:, ROWS:])
    target = lax.shift_right_logical(mine, shift)
    target_hot = ones_where(iota((NE, ROWS), 0) == target)
    before = ones_where(iota((ROWS, ROWS), 0) < iota((ROWS, ROWS), 1)).astype(BF16)
    ahead = dot(target_hot.astype(BF16), before)
    earlier = jnp.sum(target_hot * ahead, axis=0, keepdims=True).astype(jnp.int32)
    pack = ones_where(iota((NE * MC, ROWS), 0) == target * MC + earlier).astype(BF16)
    for k in range(3):
        conv_s[:, k] = dot(pack, conv_ref[k]).reshape(NE, MC, WB).astype(BF16)

    loaded(2, 3)
    ssm_f[...] = ssm_v[...].astype(F32)
    for n in range(NS):
        ssm_s[:, n] = dot(pack, ssm_f[:, n, :].astype(BF16)).reshape(NE, MC, WB).astype(BF16)

    slots = slot_ref[...]
    arriving = ones_where(lax.shift_right_logical(slots, shift) == e)
    lane = iota((LW, LW), 1)
    sub = iota((LW, LW), 0)
    before2 = ones_where((sub < lane) & ((sub < ROWS) == (lane < ROWS))).astype(BF16)
    rank = dot(arriving.astype(BF16), before2)
    place = (slots & (ROWS - 1)).astype(F32) + 1.0
    half = iota((NZ, LW), 1) >= ROWS
    to_lane = iota((NZ, NE * MC), 1) - iota((NZ, NE * MC), 0) * (2 * MC)
    spread = jnp.zeros((NZ, NE * MC), F32)
    for h in range(2):
        live = (arriving > 0.0) & (half == bool(h))
        for k in range(MC):
            found = jnp.sum(jnp.where(live & (rank == float(k)), place, 0.0), axis=1, keepdims=True)
            spread = spread + jnp.where(to_lane == h * MC + k, found, 0.0)
    row_of = jnp.sum(spread, axis=0, keepdims=True).astype(jnp.int32) - 1
    unpack = ones_where(iota((ROWS, NE * MC), 0) == row_of).astype(BF16)

    loaded(3, 5)
    r0 = rt_ref[0:1, :]
    r1 = rt_ref[1:2, :]
    g0 = gw_ref[0:1, :]
    g1 = gw_ref[1:2, :]
    expert_id = iota((NE, LW), 0)
    named = ones_where((expert_id == r0) | (expert_id == r1))
    weight = jnp.where(expert_id == r0, g0, 0.0) + jnp.where(expert_id == r1, g1, 0.0)
    w_hi = weight.astype(BF16).astype(F32)
    w_lo = weight - w_hi
    in_block = dot(named.astype(BF16), before2).astype(jnp.int32)
    seat = in_block + jnp.where(iota((NE, LW), 1) >= ROWS, CAP, 0)
    seat = jnp.where(named > 0.0, seat, -1)
    seat_id = iota((PC, LW), 0)
    rows_d, rows_hi, rows_lo = [], [], []
    for k in range(NE):
        hit = seat_id == seat[k : k + 1, :]
        rows_d.append(jnp.where(hit, 1.0, 0.0))
        rows_hi.append(jnp.where(hit, w_hi[k : k + 1, :], 0.0))
        rows_lo.append(jnp.where(hit, w_lo[k : k + 1, :], 0.0))
    disp_v[...] = jnp.concatenate(rows_d, axis=0).astype(BF16)
    dhi_v[...] = jnp.concatenate(rows_hi, axis=0).T.astype(BF16)
    dlo_v[...] = jnp.concatenate(rows_lo, axis=0).T.astype(BF16)

    def all_sent(some, ssem, rsem):
        ending.append(remote(some, some, ssem.at[0], rsem.at[0], (d, e)).wait_send)

    def all_received(some, ssem, rsem):
        remote(some, some, ssem.at[0], rsem.at[0], (d, e)).wait_recv()

    def to_experts(src_of, dst, some, ssem, rsem):
        for i in range(1, NE):
            p = (e + i) % NE
            remote(src_of(p), dst, ssem.at[0], rsem.at[0], (d, p)).start()
        all_sent(some, ssem, rsem)

    pl.semaphore_wait(barrier, NE - 1 + ND - 1)

    to_experts(lambda p: conv_s.at[p], conv_r.at[e], conv_s.at[pl.ds(0, NE - 1)], cs_sem, cr_sem)
    conv_r[e] = conv_s[e]
    ssm_r[e] = ssm_s[e]

    loaded(5, 9)
    all_received(conv_r.at[pl.ds(0, NE - 1)], cs_sem, cr_sem)
    to_experts(lambda p: ssm_s.at[p], ssm_r.at[e], ssm_s.at[pl.ds(0, NE - 1)], ss_sem, sr_sem)
    window = []
    for k in range(3):
        got = conv_r[:, k].astype(F32).reshape(NE * MC, WB).astype(BF16)
        window.append(dot(unpack, got))
    conv_o[0] = window[1].astype(BF16)
    conv_o[1] = window[2].astype(BF16)
    conv_o[2] = cin_ref[...]
    window.append(cin_ref[...].astype(F32))
    total = window[0] * cw_ref[0:1, :]
    for k in range(1, 4):
        total = total + window[k] * cw_ref[k : k + 1, :]
    activated = silu(total + cb_ref[...]).astype(BF16)
    act = activated.astype(F32)
    partial = dot_t(activated, xp_ref[...])
    RZ = ROWS // NZ
    proj_s[...] = jnp.zeros_like(proj_s)
    proj_s[:, :, : RK + 2 * NS] = partial.reshape(NZ, RZ, RK + 2 * NS)

    def proj_src(p):
        return proj_s.at[p // 2, :, pl.ds(pl.multiple_of((p % 2) * LANES, LANES), RK)]

    def to_dp(src_of, dst, some, ssem, rsem):
        for i in range(1, ND):
            p = (d + i) % ND
            remote(src_of(p), dst, ssem.at[0], rsem.at[0], (p, e)).start()
        all_sent(some, ssem, rsem)

    others = pl.ds(0, ND - 1)
    to_dp(proj_src, proj_r.at[d], proj_r.at[others], ps_sem, pr_sem)
    proj_r[d] = proj_s[z, :, pl.ds(lane0, RK)]
    store_conv = pltpu.make_async_copy(conv_o, conv_out, store_sem.at[0])
    store_conv.start()
    ending.append(store_conv.wait)

    all_received(proj_r.at[others], ps_sem, pr_sem)
    summed = proj_r[0]
    for k in range(1, ND):
        summed = summed + proj_r[k]
    proj_c[...] = summed
    to_dp(lambda p: proj_c, proj_g.at[c, z], proj_r.at[others], qs_sem, qr_sem)
    proj_g[c, z] = summed
    all_received(ssm_r.at[pl.ds(0, NE - 1)], ss_sem, sr_sem)
    for n in range(NS):
        got = ssm_r[:, n].astype(F32).reshape(NE * MC, WB).astype(BF16)
        moved_v[n] = dot(unpack, got)
    loaded(9, 14)
    gate = silu(gin_ref[...].astype(F32))
    decay = -jnp.exp(dl_ref[...])
    all_received(proj_r.at[others], qs_sem, qr_sem)
    step_low = proj_g[0].reshape(ROWS, RK)
    coef = proj_g[1][:, :, RK - LANES :].reshape(ROWS, LANES)
    mean = jnp.sum(step_low * step_low, axis=1, keepdims=True) * (1.0 / RK)
    step_norm = (step_low * lax.rsqrt(mean + 1e-06)).astype(BF16)
    pre = dot(step_norm, sw_ref[...]) + sb_ref[...]
    step = jnp.maximum(pre, 0.0) + jnp.log1p(jnp.exp(-jnp.abs(pre)))
    push = step * act

    y = sg_ref[...] * act
    read = jnp.zeros_like(y)
    for n in range(NS):
        state = jnp.exp(step * decay[n : n + 1, :]) * moved_v[n] + push * coef[:, n : n + 1]
        ssm_f[:, n, :] = state
        read = read + coef[:, NS + n : NS + n + 1] * state
    gated = ((read + y) * gate).astype(BF16)
    gat[e] = gated
    for i in range(1, NE):
        remote(gat.at[e], gat.at[e], gs_sem.at[0], gr_sem.at[e], (d, (e + i) % NE)).start()
    all_sent(gat.at[pl.ds(0, NE - 1)], gs_sem, gr_sem)
    ssm_o[...] = ssm_f[...].astype(BF16)
    store_ssm = pltpu.make_async_copy(ssm_o, ssm_out, store_sem.at[1])
    store_ssm.start()
    ending.append(store_ssm.wait)

    loaded(14, 16)
    sibling = (2 * z + 1 - c, e)

    def swap_mix(p):
        return remote(mix_s.at[1 - c, p], mix_b.at[p], bs_sem.at[0], br_sem.at[p], sibling)

    def arrived(p):
        @pl.when(p != e)
        def _():
            remote(gat.at[p], gat.at[p], gs_sem.at[0], gr_sem.at[p], (d, p)).wait_recv()

    def project(p):
        arrived(2 * p)
        arrived(2 * p + 1)
        mixed = dot(gat[pl.ds(2 * p, 2)].reshape(LW, WB), wo_ref[...])
        mix_s[0, p] = mixed[:, :LANES].astype(BF16)
        mix_s[1, p] = mixed[:, LANES:].astype(BF16)
        swap_mix(p).start()

    def send_mix(i):
        p = (z + i) % NZ
        return remote(mix_t.at[p], mix_r.at[z], ms_sem.at[0], mr_sem.at[0], (2 * p + c, e))

    def join(i):
        p = (z + i) % NZ
        swap_mix(p).wait_recv()
        mix_t[p] = (mix_s[c, p].astype(F32) + mix_b[p].astype(F32)).astype(BF16)
        if i > 0:
            send_mix(i).start()

    all_sent(mix_b, bs_sem, br_sem)
    order = [*range(1, NZ), 0]
    for at, i in enumerate(order):
        project((z + i) % NZ)
        if at > 0:
            join(order[at - 1])
    join(0)
    mix_r[z] = mix_t[z]
    all_sent(mix_t.at[pl.ds(0, NZ - 1)], ms_sem, mr_sem)

    all_received(mix_r.at[pl.ds(0, NZ - 1)], ms_sem, mr_sem)
    mixed = mix_r[0].astype(F32)
    for k in range(1, NZ):
        mixed = mixed + mix_r[k].astype(F32)
    stream = (res_v[...].astype(F32) + mixed).astype(BF16)
    stream_v[...] = stream

    disp_s[...] = dot(disp_v[...], stream).reshape(NE, PC, LANES).astype(BF16)
    to_experts(lambda p: disp_s.at[p], xb.at[c, z, e], disp_s.at[pl.ds(0, NE - 1)], ds_sem, dr_sem)
    xb[c, z, e] = disp_s[e]
    all_received(disp_s.at[pl.ds(0, NE - 1)], ds_sem, dr_sem)

    right = (2 * ((z + 1) % NZ) + c, e)
    left = (2 * ((z + NZ - 1) % NZ) + c, e)
    far = NZ // 2
    pieces = range(NP)
    hops_r = [far if h < NP // 2 else NZ - 1 - far for h in pieces]
    hops_l = [NZ - 1 - far if h < NP // 2 else far for h in pieces]
    halves = [pl.ds(h * HE, HE) for h in pieces]

    def back(s):
        return (z + NZ - s) % NZ

    def ahead_z(s):
        return (z + s) % NZ

    def ring_right(h, s):
        p = back(s)
        part = xb.at[c, p, halves[h]]
        return remote(part, part, xrs.at[h, s], xrr.at[h, s], right)

    def ring_left(h, s):
        p = ahead_z(s)
        part = xb.at[c, p, halves[h]]
        return remote(part, part, xls.at[h, s], xlr.at[h, s], left)

    def wait_right(h, s):
        part = xb.at[c, back(s + 1), halves[h]]
        remote(part, part, xrs.at[h, s], xrr.at[h, s], right).wait_recv()

    def wait_left(h, s):
        part = xb.at[c, ahead_z(s + 1), halves[h]]
        remote(part, part, xls.at[h, s], xlr.at[h, s], left).wait_recv()

    def over(p):
        return remote(xb.at[c, p], xb.at[c, p], xss.at[0], xsr.at[p], sibling)

    def wait_over(p):
        remote(xb.at[1 - c, p], xb.at[1 - c, p], xss.at[0], xsr.at[p], sibling).wait_recv()

    all_sent(xb.at[0], xss, xsr)

    def normalise(o, p):
        square = jnp.zeros((PC, LANES), F32)
        for k in range(NE):
            for m in range(2):
                v = xb[m, p, k].astype(F32)
                square = square + v * v
        scale = lax.rsqrt(jnp.sum(square, axis=1, keepdims=True) * (1.0 / D) + 1e-05)
        for k in range(NE):
            for m in range(2):
                v = xb[m, p, k].astype(F32) * scale * ng_ref[2 * k + m : 2 * k + m + 1, :]
                if MP > PC:
                    v = jnp.concatenate([v, jnp.zeros((MP - PC, LANES), F32)], axis=0)
                xn[o, :, (2 * k + m) * LANES : (2 * k + m + 1) * LANES] = v.astype(BF16)

    steps = [[(0, z, 0)]]
    for s in range(1, far):
        steps.append([(2 * s - 1, back(s), -s), (2 * s, ahead_z(s), s)])
    steps.append([(NZ - 1, ahead_z(far), far)])
    number = {off % NZ: o for group in steps for o, _, off in group}
    FIRST = sum(len(group) for group in steps[: max(1, far - 1)])
    KC = min(D, 1024)

    def gate_up(lo, hi):
        rows = pl.ds(lo * MP, (hi - lo) * MP)
        acc_g[rows] = jnp.zeros(((hi - lo) * MP, acc_g.shape[1]), F32)
        acc_u[rows] = jnp.zeros(((hi - lo) * MP, acc_u.shape[1]), F32)

        def depth(k):
            at = pl.ds(pl.multiple_of(k * KC, KC), KC)
            x = xn[lo:hi, :, at].reshape((hi - lo) * MP, KC)
            acc_g[rows] += dot_t(x, wg_v[:, at])
            acc_u[rows] += dot_t(x, wu_v[:, at])

        times(0, D // KC, depth)
        hid[rows] = (silu(acc_g[rows]) * acc_u[rows]).astype(BF16)

    def settle(group):
        for o, p, _ in group:
            wait_over(p)
            normalise(o, p)

    loaded(16, 19)
    for s in range(far + 1):
        for h in pieces:
            if 0 < s <= hops_r[h]:
                wait_right(h, s - 1)
            if s < hops_r[h]:
                go(ring_right(h, s))
            if 0 < s <= hops_l[h]:
                wait_left(h, s - 1)
            if s < hops_l[h]:
                go(ring_left(h, s))
        for _, p, _ in steps[s]:
            over(p).start()
        if s > 0:
            settle(steps[s - 1])
        if s == max(1, far - 1):
            gate_up(0, FIRST)
    settle(steps[far])
    gate_up(FIRST, NZ)
    loaded(19, 20)

    def down(lo, hi):
        def one(k):
            at = pl.ds(pl.multiple_of(k * WB, WB), WB)
            out = dot(hid[lo * MP : hi * MP], wd_v[:, at]).reshape(hi - lo, MP, WB)[:, :PC].astype(BF16)
            yp[0, lo:hi, k] = out[:, :, :LANES]
            yp[1, lo:hi, k] = out[:, :, LANES:]

        times(0, NE, one)

    def swap_y(g):
        lo, hi = ((FIRST, NZ), (0, FIRST))[g]
        part = pl.ds(lo, hi - lo)
        return remote(yp.at[1 - c, part], ysib.at[part], yss_sem.at[g], ysr_sem.at[g], sibling)

    down(FIRST, NZ)
    go(swap_y(0))

    def own(h, off):
        o = number[off % NZ]
        return yp[c, o, h * HE : (h + 1) * HE].astype(F32) + ysib[o, h * HE : (h + 1) * HE].astype(F32)

    def chain_right(h, s):
        return remote(yrs.at[h, s], yrr.at[h, s], yrs_sem.at[h, s], yrr_sem.at[h, s], right)

    def chain_left(h, s):
        return remote(yls.at[h, s], ylr.at[h, s], yls_sem.at[h, s], ylr_sem.at[h, s], left)

    def chain_step(h, s):
        if s < hops_r[h]:
            part = own(h, hops_r[h] - s)
            if s > 0:
                chain_right(h, s - 1).wait_recv()
                part = part + yrr[h, s - 1].astype(F32)
            yrs[h, s] = part.astype(BF16)
            go(chain_right(h, s))
        if s < hops_l[h]:
            part = own(h, s - hops_l[h])
            if s > 0:
                chain_left(h, s - 1).wait_recv()
                part = part + ylr[h, s - 1].astype(F32)
            yls[h, s] = part.astype(BF16)
            go(chain_left(h, s))

    swap_y(0).wait_recv()
    if FIRST <= NZ - 3:
        for h in pieces:
            chain_step(h, 0)
        down(0, FIRST)
        go(swap_y(1))
        swap_y(1).wait_recv()
    else:
        down(0, FIRST)
        go(swap_y(1))
        swap_y(1).wait_recv()
        for h in pieces:
            chain_step(h, 0)
    for s in range(1, far):
        for h in pieces:
            chain_step(h, s)
    def returned(k):
        return remote(ret_s.at[k], ret_r.at[e], rs_sem.at[0], rr_sem.at[0], (d, k))

    def give_back(k):
        @pl.when(e != k)
        def _():
            returned(k).start()

        @pl.when(e == k)
        def _():
            ret_r[k] = ret_s[k]

    all_sent(ret_s.at[pl.ds(0, NE - 1)], rs_sem, rr_sem)
    for h in pieces:
        part = own(h, 0)
        if hops_r[h] > 0:
            chain_right(h, hops_r[h] - 1).wait_recv()
            part = part + yrr[h, hops_r[h] - 1].astype(F32)
        if hops_l[h] > 0:
            chain_left(h, hops_l[h] - 1).wait_recv()
            part = part + ylr[h, hops_l[h] - 1].astype(F32)
        ret_s[h * HE : (h + 1) * HE] = part.astype(BF16)
        for k in range(h * HE, (h + 1) * HE):
            give_back(k)

    all_received(ret_r.at[pl.ds(0, NE - 1)], rs_sem, rr_sem)
    back_rows = ret_r[...].astype(F32).reshape(NE * PC, LANES).astype(BF16)
    final = stream_v[...].astype(F32) + dot(dhi_v[...], back_rows) + dot(dlo_v[...], back_rows)
    outg[c, z] = final.astype(BF16)

    def send_out(i):
        p = (z + i) % NZ
        return remote(outg.at[c, z], outg.at[c, z], os_sem.at[0], or_sem.at[z], (2 * p + c, e))

    def wait_out(i):
        p = (z + NZ - i) % NZ
        remote(outg.at[c, p], outg.at[c, p], os_sem.at[i], or_sem.at[p], (2 * p + c, e)).wait_recv()

    def pass_out(p):
        return remote(outg.at[c, p], outg.at[c, p], ts_sem.at[0], tr_sem.at[p], sibling)

    times(1, NZ, lambda i: send_out(i).start())
    all_sent(outg.at[0, pl.ds(0, NZ - 1)], os_sem, or_sem)
    pass_out(z).start()
    all_sent(outg.at[0], ts_sem, tr_sem)

    def relay(i):
        wait_out(i)
        pass_out((z + NZ - i) % NZ).start()

    times(1, NZ, relay)

    def store_out(m, p):
        at = layer_out.at[pl.ds(pl.multiple_of(p * LW, LW), LW), pl.ds(pl.multiple_of(m * LANES, LANES), LANES)]
        return pltpu.make_async_copy(outg.at[m, p], at, out_sem.at[m, p])

    def wait_pass(i):
        p = (z + NZ - i) % NZ
        remote(outg.at[1 - c, p], outg.at[1 - c, p], ts_sem.at[p], tr_sem.at[p], sibling).wait_recv()
        store_out(c, p).start()
        store_out(1 - c, p).start()

    times(0, NZ, wait_pass)

    def stored(p):
        store_out(c, p).wait()
        store_out(1 - c, p).wait()

    times(0, NZ, stored)

    for wait in ending:
        wait()


def hand_over(a, b, c, oa, ob, oc, va, vb, vc, sem):
    through = ((a, va, oa), (b, vb, ob), (c, vc, oc))
    first = [pltpu.make_async_copy(x, v, sem.at[i]) for i, (x, v, _) in enumerate(through)]
    second = [pltpu.make_async_copy(v, y, sem.at[i]) for i, (_, v, y) in enumerate(through)]
    for copy in first:
        copy.start()
    for one, two in zip(first, second):
        one.wait()
        two.start()
    for copy in second:
        copy.wait()


def body(
    ssm_state, conv_state, new_slot, conv_input, gate_input, conv_weight, conv_bias, x_proj_weight,
    step_weight, step_bias, decay_log, skip_gain, out_proj_weight, residual, norm_gain, routes,
    gate_weight, expert_gate, expert_up, expert_down,
):
    ROWS, NS, WB = ssm_state.shape
    NE = lax.axis_size("expert")
    NZ = lax.axis_size("dp") // 2
    RK = step_weight.shape[0]
    FB = expert_gate.shape[2]
    MC = 2 * ROWS // NE
    CAP = min(ROWS, 5 * ROWS * routes.shape[1] // (2 * NE))
    PC, LW, D, NP = 2 * CAP, 2 * ROWS, NE * WB, 4
    HE = NE // NP
    MP = (PC + 15) // 16 * 16
    RZ = ROWS // NZ
    far = NZ // 2
    hbm = pl.BlockSpec(memory_space=pl.ANY)
    V, S = pltpu.VMEM, pltpu.SemaphoreType.DMA
    scratch = [
        V((3, ROWS, WB), BF16), V((NZ, LW), jnp.int32), V((ROWS, WB), BF16), V((ROWS, WB), BF16),
        V((4, WB), F32), V((1, WB), F32), V((RK + 2 * NS, WB), BF16), V((RK, WB), BF16), V((1, WB), F32),
        V((NS, WB), F32), V((1, WB), F32), V((WB, WB), BF16), V((2 * NE, LANES), F32),
        V((2, LW), jnp.int32), V((2, LW), F32),
        V((ROWS, NS, WB), BF16), V((ROWS, NS, WB), F32), V((NS, ROWS, WB), F32), V((LW, LANES), BF16),
        V((FB, D), BF16), V((FB, D), BF16), V((FB, D), BF16),
        V((NE, 3, MC, WB), BF16), V((NE, 3, MC, WB), BF16),
        V((NE, NS, MC, WB), BF16), V((NE, NS, MC, WB), BF16),
        V((ROWS, NS, WB), BF16), V((3, ROWS, WB), BF16),
        V((NZ, RZ, RK + LANES), F32), V((2 * NZ, RZ, RK), F32), V((RZ, RK), F32), V((2, NZ, RZ, RK), F32),
        V((NE, ROWS, WB), BF16), V((2, NZ, LW, LANES), BF16), V((NZ, LW, LANES), BF16),
        V((NZ, LW, LANES), BF16), V((NZ, LW, LANES), BF16), V((LW, LANES), BF16),
        V((NE, PC, LANES), BF16), V((2, NZ, NE, PC, LANES), BF16), V((NZ, MP, D), BF16),
        V((NZ * MP, FB), F32), V((NZ * MP, FB), F32), V((NZ * MP, FB), BF16),
        V((2, NZ, NE, PC, LANES), BF16), V((NZ, NE, PC, LANES), BF16),
        V((NP, far, HE, PC, LANES), BF16), V((NP, far, HE, PC, LANES), BF16),
        V((NP, far, HE, PC, LANES), BF16), V((NP, far, HE, PC, LANES), BF16),
        V((NE, PC, LANES), BF16), V((NE, PC, LANES), BF16),
        V((NE * PC, LW), BF16), V((LW, NE * PC), BF16), V((LW, NE * PC), BF16), V((2, NZ, LW, LANES), BF16),
        S((20,)), S((NE,)), S((NE,)), S((NE,)), S((NE,)), S((2,)),
        S((2 * NZ,)), S((2 * NZ,)), S((2 * NZ,)), S((2 * NZ,)), S((NE,)), S((NE,)),
        S((NZ,)), S((NZ,)), S((NZ,)), S((NZ,)), S((NE,)), S((NE,)),
        S((NP, far)), S((NP, far)), S((NP, far)), S((NP, far)), S((NZ,)), S((NZ,)),
        S((2,)), S((2,)), S((NP, far)), S((NP, far)), S((NP, far)), S((NP, far)),
        S((NE,)), S((NE,)), S((NZ,)), S((NZ,)), S((NZ,)), S((NZ,)), S((2, NZ)),
    ]
    call = pl.pallas_call(
        functools.partial(kernel, (NE, NZ, ROWS, MC, CAP)),
        out_shape=(
            jax.ShapeDtypeStruct((ROWS, NS, WB), BF16),
            jax.ShapeDtypeStruct((3, ROWS, WB), BF16),
            jax.ShapeDtypeStruct((NE * ROWS, WB), BF16),
        ),
        in_specs=[hbm] * 20,
        out_specs=(hbm, hbm, hbm),
        scratch_shapes=scratch,
        compiler_params=pltpu.CompilerParams(
            collective_id=0, has_side_effects=True, vmem_limit_bytes=56 * 1024 * 1024
        ),
        name="decode_step",
    )
    ssm_new, conv_new, layer = call(
        ssm_state, conv_state.transpose(1, 0, 2), new_slot.reshape(NZ, LW), conv_input, gate_input,
        conv_weight, conv_bias.reshape(1, WB), x_proj_weight.T, step_weight, step_bias.reshape(1, WB),
        decay_log, skip_gain.reshape(1, WB), out_proj_weight, residual, norm_gain.reshape(2 * NE, LANES),
        routes.T, gate_weight.T, expert_gate[0].T, expert_up[0].T, expert_down[0],
    )
    shapes = [jax.ShapeDtypeStruct(v.shape, v.dtype) for v in (ssm_new, conv_new, layer)]
    ssm_new, conv_new, layer = pl.pallas_call(
        hand_over, out_shape=shapes, in_specs=[hbm] * 3, out_specs=[hbm] * 3, scratch_shapes=[*(V(v.shape, v.dtype) for v in shapes), S((3,))], name="hand_over"
    )(ssm_new, conv_new, layer)
    return ssm_new, conv_new.transpose(1, 0, 2), layer


def solution(mesh):
    in_specs = (
        P("expert", None, "dp"), P("expert", None, "dp"), P(), P("expert", "dp"), P("expert", "dp"),
        P(None, "dp"), P("dp"), P("dp", None), P(None, "dp"), P("dp"), P(None, "dp"), P("dp"),
        P("dp", "expert"), P(None, "expert"), P(), P(), P(),
        P("expert", None, "dp"), P("expert", None, "dp"), P("expert", "dp", None),
    )
    out_specs = (P("expert", None, "dp"), P("expert", None, "dp"), P(None, "expert"))
    return jax.shard_map(body, mesh=mesh, in_specs=in_specs, out_specs=out_specs, check_vma=False)
```

```python
import functools

import jax
import jax.numpy as jnp
from jax import lax
from jax.experimental import pallas as pl
from jax.experimental.pallas import tpu as pltpu
from jax.sharding import PartitionSpec as P

MESH = pl.DeviceIdType.MESH
F32 = jnp.float32
BF16 = jnp.bfloat16
LANES = 128


def iota(shape, axis):
    return lax.broadcasted_iota(jnp.int32, shape, axis)


def ones_where(mask):
    return jnp.where(mask, 1.0, 0.0)


def dot(a, b):
    return jnp.dot(a, b, preferred_element_type=F32)


def dot_t(a, b):
    return lax.dot_general(a, b, (((1,), (1,)), ((), ())), preferred_element_type=F32)


def silu(v):
    return v / (1.0 + jnp.exp(-v))


def times(lo, hi, step):
    def run(i, carry):
        step(i)
        return carry

    lax.fori_loop(lo, hi, run, 0)


def kernel(
    dims,
    ssm_hbm, conv_hbm, slot_hbm, cin_hbm, gin_hbm, cw_hbm, cb_hbm, xp_hbm, sw_hbm, sb_hbm,
    dl_hbm, sg_hbm, wo_hbm, res_hbm, ng_hbm, rt_hbm, gw_hbm, wg_hbm, wu_hbm, wd_hbm,
    ssm_out, conv_out, layer_out,
    conv_ref, slot_ref, cin_ref, gin_ref, cw_ref, cb_ref, xp_ref, sw_ref, sb_ref,
    dl_ref, sg_ref, wo_ref, ng_ref, rt_ref, gw_ref,
    ssm_v, ssm_f, moved_v, res_v, wg_v, wu_v, wd_v,
    conv_s, conv_r, ssm_s, ssm_r, ssm_o, conv_o,
    proj_s, proj_r, proj_c, proj_g,
    gat, mix_s, mix_b, mix_t, mix_r, stream_v,
    disp_s, xb, xn, acc_g, acc_u, hid, yp, ysib, yrs, yrr, yls, ylr,
    ret_s, ret_r, disp_v, dhi_v, dlo_v, outg,
    load_sem, cs_sem, cr_sem, ss_sem, sr_sem, store_sem,
    ps_sem, pr_sem, qs_sem, qr_sem, gs_sem, gr_sem,
    ms_sem, mr_sem, bs_sem, br_sem, ds_sem, dr_sem,
    xs_sem, xrr, xlr, xss, xsr,
    yss_sem, ysr_sem, ys_sem, yrr_sem, ylr_sem,
    rs_sem, rr_sem, os_sem, or_sem, ts_sem, tr_sem, out_sem, fs_sem, fr_sem,
):
    NE, NZ, ROWS, MC, CAP = dims
    ND = 2 * NZ
    PC = 2 * CAP
    LW = 2 * ROWS
    NS = dl_ref.shape[0]
    WB = cin_ref.shape[1]
    RK = sw_ref.shape[0]
    D = NE * WB
    NP = yrs.shape[0]
    HE = NE // NP
    MP = xn.shape[1]
    shift = ROWS.bit_length() - 1
    d = lax.axis_index("dp")
    e = lax.axis_index("expert")
    z = d // 2
    c = d % 2

    def remote(src, dst, ssem, rsem, dev):
        return pltpu.make_async_remote_copy(
            src_ref=src, dst_ref=dst, send_sem=ssem, recv_sem=rsem, device_id=dev, device_id_type=MESH
        )

    ending = []

    barrier = pltpu.get_barrier_semaphore()
    for i in range(1, ND):
        pl.semaphore_signal(barrier, inc=1, device_id=((d + i) % ND, e), device_id_type=MESH)
    for i in range(1, NE):
        pl.semaphore_signal(barrier, inc=1, device_id=(d, (e + i) % NE), device_id_type=MESH)

    row0 = pl.multiple_of(z * LW, LW)
    lane0 = pl.multiple_of(c * LANES, LANES)
    pair = pl.ds(row0, LW)
    sources = [
        (conv_hbm, conv_ref), (slot_hbm, slot_ref), (ssm_hbm, ssm_v), (rt_hbm.at[:, pair], rt_ref),
        (gw_hbm.at[:, pair], gw_ref), (cin_hbm, cin_ref), (cw_hbm, cw_ref), (cb_hbm, cb_ref), (xp_hbm, xp_ref),
        (sw_hbm, sw_ref), (sb_hbm, sb_ref), (dl_hbm, dl_ref), (sg_hbm, sg_ref), (gin_hbm, gin_ref), (wo_hbm, wo_ref),
        (res_hbm.at[pair, pl.ds(lane0, LANES)], res_v), (ng_hbm, ng_ref), (wg_hbm, wg_v), (wu_hbm, wu_v), (wd_hbm, wd_v),
    ]
    loads = [pltpu.make_async_copy(src, dst, load_sem.at[i]) for i, (src, dst) in enumerate(sources)]
    for load in loads:
        load.start()

    def loaded(lo, hi):
        for load in loads[lo:hi]:
            load.wait()

    loaded(0, 2)

    mine = slot_ref[pl.ds(e // 2, 1), :]
    mine = jnp.where(e % 2 == 0, mine[:, :ROWS], mine[:, ROWS:])
    target = lax.shift_right_logical(mine, shift)
    target_hot = ones_where(iota((NE, ROWS), 0) == target)
    before = ones_where(iota((ROWS, ROWS), 0) < iota((ROWS, ROWS), 1)).astype(BF16)
    ahead = dot(target_hot.astype(BF16), before)
    earlier = jnp.sum(target_hot * ahead, axis=0, keepdims=True).astype(jnp.int32)
    pack = ones_where(iota((NE * MC, ROWS), 0) == target * MC + earlier).astype(BF16)
    for k in range(3):
        conv_s[:, k] = dot(pack, conv_ref[k]).reshape(NE, MC, WB).astype(BF16)

    loaded(2, 3)
    ssm_f[...] = ssm_v[...].astype(F32)
    for n in range(NS):
        ssm_s[:, n] = dot(pack, ssm_f[:, n, :].astype(BF16)).reshape(NE, MC, WB).astype(BF16)

    slots = slot_ref[...]
    arriving = ones_where(lax.shift_right_logical(slots, shift) == e)
    lane = iota((LW, LW), 1)
    sub = iota((LW, LW), 0)
    before2 = ones_where((sub < lane) & ((sub < ROWS) == (lane < ROWS))).astype(BF16)
    rank = dot(arriving.astype(BF16), before2)
    place = (slots & (ROWS - 1)).astype(F32) + 1.0
    half = iota((NZ, LW), 1) >= ROWS
    to_lane = iota((NZ, NE * MC), 1) - iota((NZ, NE * MC), 0) * (2 * MC)
    spread = jnp.zeros((NZ, NE * MC), F32)
    for h in range(2):
        live = (arriving > 0.0) & (half == bool(h))
        for k in range(MC):
            found = jnp.sum(jnp.where(live & (rank == float(k)), place, 0.0), axis=1, keepdims=True)
            spread = spread + jnp.where(to_lane == h * MC + k, found, 0.0)
    row_of = jnp.sum(spread, axis=0, keepdims=True).astype(jnp.int32) - 1
    unpack = ones_where(iota((ROWS, NE * MC), 0) == row_of).astype(BF16)

    loaded(3, 5)
    r0 = rt_ref[0:1, :]
    r1 = rt_ref[1:2, :]
    g0 = gw_ref[0:1, :]
    g1 = gw_ref[1:2, :]
    expert_id = iota((NE, LW), 0)
    named = ones_where((expert_id == r0) | (expert_id == r1))
    weight = jnp.where(expert_id == r0, g0, 0.0) + jnp.where(expert_id == r1, g1, 0.0)
    w_hi = weight.astype(BF16).astype(F32)
    w_lo = weight - w_hi
    in_block = dot(named.astype(BF16), before2).astype(jnp.int32)
    seat = in_block + jnp.where(iota((NE, LW), 1) >= ROWS, CAP, 0)
    seat = jnp.where(named > 0.0, seat, -1)
    seat_id = iota((PC, LW), 0)
    rows_d, rows_hi, rows_lo = [], [], []
    for k in range(NE):
        hit = seat_id == seat[k : k + 1, :]
        rows_d.append(jnp.where(hit, 1.0, 0.0))
        rows_hi.append(jnp.where(hit, w_hi[k : k + 1, :], 0.0))
        rows_lo.append(jnp.where(hit, w_lo[k : k + 1, :], 0.0))
    disp_v[...] = jnp.concatenate(rows_d, axis=0).astype(BF16)
    dhi_v[...] = jnp.concatenate(rows_hi, axis=0).T.astype(BF16)
    dlo_v[...] = jnp.concatenate(rows_lo, axis=0).T.astype(BF16)

    def all_sent(some, ssem, rsem):
        ending.append(remote(some, some, ssem.at[0], rsem.at[0], (d, e)).wait_send)

    def all_received(some, ssem, rsem):
        remote(some, some, ssem.at[0], rsem.at[0], (d, e)).wait_recv()

    def to_experts(src_of, dst, some, ssem, rsem):
        for i in range(1, NE):
            p = (e + i) % NE
            remote(src_of(p), dst, ssem.at[0], rsem.at[0], (d, p)).start()
        all_sent(some, ssem, rsem)

    pl.semaphore_wait(barrier, NE - 1 + ND - 1)

    to_experts(lambda p: conv_s.at[p], conv_r.at[e], conv_s.at[pl.ds(0, NE - 1)], cs_sem, cr_sem)
    conv_r[e] = conv_s[e]
    ssm_r[e] = ssm_s[e]

    loaded(5, 9)
    all_received(conv_r.at[pl.ds(0, NE - 1)], cs_sem, cr_sem)
    to_experts(lambda p: ssm_s.at[p], ssm_r.at[e], ssm_s.at[pl.ds(0, NE - 1)], ss_sem, sr_sem)
    window = []
    for k in range(3):
        got = conv_r[:, k].astype(F32).reshape(NE * MC, WB).astype(BF16)
        window.append(dot(unpack, got))
    conv_o[0] = window[1].astype(BF16)
    conv_o[1] = window[2].astype(BF16)
    conv_o[2] = cin_ref[...]
    window.append(cin_ref[...].astype(F32))
    total = window[0] * cw_ref[0:1, :]
    for k in range(1, 4):
        total = total + window[k] * cw_ref[k : k + 1, :]
    activated = silu(total + cb_ref[...]).astype(BF16)
    act = activated.astype(F32)
    partial = dot_t(activated, xp_ref[...])
    RZ = ROWS // NZ
    proj_s[...] = jnp.zeros_like(proj_s)
    proj_s[:, :, : RK + 2 * NS] = partial.reshape(NZ, RZ, RK + 2 * NS)

    def proj_src(p):
        return proj_s.at[p // 2, :, pl.ds(pl.multiple_of((p % 2) * LANES, LANES), RK)]

    def to_dp(src_of, dst, some, ssem, rsem):
        for i in range(1, ND):
            p = (d + i) % ND
            remote(src_of(p), dst, ssem.at[0], rsem.at[0], (p, e)).start()
        all_sent(some, ssem, rsem)

    others = pl.ds(0, ND - 1)
    to_dp(proj_src, proj_r.at[d], proj_r.at[others], ps_sem, pr_sem)
    proj_r[d] = proj_s[z, :, pl.ds(lane0, RK)]
    store_conv = pltpu.make_async_copy(conv_o, conv_out, store_sem.at[0])
    store_conv.start()
    ending.append(store_conv.wait)

    all_received(proj_r.at[others], ps_sem, pr_sem)
    summed = proj_r[0]
    for k in range(1, ND):
        summed = summed + proj_r[k]
    proj_c[...] = summed
    to_dp(lambda p: proj_c, proj_g.at[c, z], proj_r.at[others], qs_sem, qr_sem)
    proj_g[c, z] = summed
    all_received(ssm_r.at[pl.ds(0, NE - 1)], ss_sem, sr_sem)
    for n in range(NS):
        got = ssm_r[:, n].astype(F32).reshape(NE * MC, WB).astype(BF16)
        moved_v[n] = dot(unpack, got)
    loaded(9, 14)
    gate = silu(gin_ref[...].astype(F32))
    decay = -jnp.exp(dl_ref[...])
    all_received(proj_r.at[others], qs_sem, qr_sem)
    step_low = proj_g[0].reshape(ROWS, RK)
    coef = proj_g[1][:, :, RK - LANES :].reshape(ROWS, LANES)
    mean = jnp.sum(step_low * step_low, axis=1, keepdims=True) * (1.0 / RK)
    step_norm = (step_low * lax.rsqrt(mean + 1e-06)).astype(BF16)
    pre = dot(step_norm, sw_ref[...]) + sb_ref[...]
    step = jnp.maximum(pre, 0.0) + jnp.log1p(jnp.exp(-jnp.abs(pre)))
    push = step * act

    y = sg_ref[...] * act
    read = jnp.zeros_like(y)
    for n in range(NS):
        state = jnp.exp(step * decay[n : n + 1, :]) * moved_v[n] + push * coef[:, n : n + 1]
        ssm_f[:, n, :] = state
        read = read + coef[:, NS + n : NS + n + 1] * state
    gated = ((read + y) * gate).astype(BF16)
    gat[e] = gated
    for i in range(1, NE):
        remote(gat.at[e], gat.at[e], gs_sem.at[0], gr_sem.at[e], (d, (e + i) % NE)).start()
    all_sent(gat.at[pl.ds(0, NE - 1)], gs_sem, gr_sem)
    ssm_o[...] = ssm_f[...].astype(BF16)
    store_ssm = pltpu.make_async_copy(ssm_o, ssm_out, store_sem.at[1])
    store_ssm.start()
    ending.append(store_ssm.wait)

    loaded(14, 16)
    sibling = (2 * z + 1 - c, e)

    def swap_mix(p):
        return remote(mix_s.at[1 - c, p], mix_b.at[p], bs_sem.at[0], br_sem.at[p], sibling)

    def arrived(p):
        @pl.when(p != e)
        def _():
            remote(gat.at[p], gat.at[p], gs_sem.at[0], gr_sem.at[p], (d, p)).wait_recv()

    def project(p):
        arrived(2 * p)
        arrived(2 * p + 1)
        mixed = dot(gat[pl.ds(2 * p, 2)].reshape(LW, WB), wo_ref[...])
        mix_s[0, p] = mixed[:, :LANES].astype(BF16)
        mix_s[1, p] = mixed[:, LANES:].astype(BF16)
        swap_mix(p).start()

    def send_mix(i):
        p = (z + i) % NZ
        return remote(mix_t.at[p], mix_r.at[z], ms_sem.at[0], mr_sem.at[0], (2 * p + c, e))

    def join(i):
        p = (z + i) % NZ
        swap_mix(p).wait_recv()
        mix_t[p] = (mix_s[c, p].astype(F32) + mix_b[p].astype(F32)).astype(BF16)
        if i > 0:
            send_mix(i).start()

    all_sent(mix_b, bs_sem, br_sem)
    order = [*range(1, NZ), 0]
    for at, i in enumerate(order):
        project((z + i) % NZ)
        if at > 0:
            join(order[at - 1])
    join(0)
    mix_r[z] = mix_t[z]
    all_sent(mix_t.at[pl.ds(0, NZ - 1)], ms_sem, mr_sem)

    all_received(mix_r.at[pl.ds(0, NZ - 1)], ms_sem, mr_sem)
    mixed = mix_r[0].astype(F32)
    for k in range(1, NZ):
        mixed = mixed + mix_r[k].astype(F32)
    stream = (res_v[...].astype(F32) + mixed).astype(BF16)
    stream_v[...] = stream

    disp_s[...] = dot(disp_v[...], stream).reshape(NE, PC, LANES).astype(BF16)
    to_experts(lambda p: disp_s.at[p], xb.at[c, z, e], disp_s.at[pl.ds(0, NE - 1)], ds_sem, dr_sem)
    xb[c, z, e] = disp_s[e]
    all_received(disp_s.at[pl.ds(0, NE - 1)], ds_sem, dr_sem)

    right = (2 * ((z + 1) % NZ) + c, e)
    left = (2 * ((z + NZ - 1) % NZ) + c, e)
    far = NZ // 2
    pieces = range(NP)
    hops_r = [far if h < NP // 2 else NZ - 1 - far for h in pieces]
    hops_l = [NZ - 1 - far if h < NP // 2 else far for h in pieces]
    halves = [pl.ds(h * HE, HE) for h in pieces]

    def back(s):
        return (z + NZ - s) % NZ

    def ahead_z(s):
        return (z + s) % NZ

    def ring_right(h, s):
        p = back(s)
        part = xb.at[c, p, halves[h]]
        return remote(part, part, xs_sem.at[0], xrr.at[h, s], right)

    def ring_left(h, s):
        p = ahead_z(s)
        part = xb.at[c, p, halves[h]]
        return remote(part, part, xs_sem.at[0], xlr.at[h, s], left)

    def wait_right(h, s):
        part = xb.at[c, back(s + 1), halves[h]]
        remote(part, part, xs_sem.at[0], xrr.at[h, s], right).wait_recv()

    def wait_left(h, s):
        part = xb.at[c, ahead_z(s + 1), halves[h]]
        remote(part, part, xs_sem.at[0], xlr.at[h, s], left).wait_recv()

    def over(p):
        return remote(xb.at[c, p], xb.at[c, p], xss.at[0], xsr.at[p], sibling)

    def wait_over(p):
        remote(xb.at[1 - c, p], xb.at[1 - c, p], xss.at[0], xsr.at[p], sibling).wait_recv()

    all_sent(xb.at[0], xss, xsr)
    all_sent(xb.at[0, pl.ds(0, NZ - 1)], xs_sem, xss)

    def normalise(o, p):
        square = jnp.zeros((PC, LANES), F32)
        for k in range(NE):
            for m in range(2):
                v = xb[m, p, k].astype(F32)
                square = square + v * v
        scale = lax.rsqrt(jnp.sum(square, axis=1, keepdims=True) * (1.0 / D) + 1e-05)
        for k in range(NE):
            for m in range(2):
                v = xb[m, p, k].astype(F32) * scale * ng_ref[2 * k + m : 2 * k + m + 1, :]
                if MP > PC:
                    v = jnp.concatenate([v, jnp.zeros((MP - PC, LANES), F32)], axis=0)
                xn[o, :, (2 * k + m) * LANES : (2 * k + m + 1) * LANES] = v.astype(BF16)

    steps = [[(0, z, 0)]]
    for s in range(1, far):
        steps.append([(2 * s - 1, back(s), -s), (2 * s, ahead_z(s), s)])
    steps.append([(NZ - 1, ahead_z(far), far)])
    number = {off % NZ: o for group in steps for o, _, off in group}
    FIRST = sum(len(group) for group in steps[: max(1, far - 1)])
    KC = min(D, 1024)

    def gate_up(lo, hi):
        rows = pl.ds(lo * MP, (hi - lo) * MP)
        acc_g[rows] = jnp.zeros(((hi - lo) * MP, acc_g.shape[1]), F32)
        acc_u[rows] = jnp.zeros(((hi - lo) * MP, acc_u.shape[1]), F32)

        def depth(k):
            at = pl.ds(pl.multiple_of(k * KC, KC), KC)
            x = xn[lo:hi, :, at].reshape((hi - lo) * MP, KC)
            acc_g[rows] += dot_t(x, wg_v[:, at])
            acc_u[rows] += dot_t(x, wu_v[:, at])

        times(0, D // KC, depth)
        hid[rows] = (silu(acc_g[rows]) * acc_u[rows]).astype(BF16)

    def settle(group):
        for o, p, _ in group:
            wait_over(p)
            normalise(o, p)

    loaded(16, 19)
    def ring_step(s, lead):
        for h in pieces:
            if (h < NP // 2) == lead:
                if 0 < s <= hops_r[h]:
                    wait_right(h, s - 1)
                if s < hops_r[h]:
                    ring_right(h, s).start()
            else:
                if 0 < s <= hops_l[h]:
                    wait_left(h, s - 1)
                if s < hops_l[h]:
                    ring_left(h, s).start()

    for s in range(far + 1):
        ring_step(s, True)
        if s == 0:
            over(z).start()
            settle(steps[0])
        ring_step(s, False)
        if s > 0:
            for _, p, _ in steps[s]:
                over(p).start()
        if 0 < s < far - 1:
            settle(steps[s])
        if s == max(1, far - 1):
            gate_up(0, FIRST)
    if far > 1:
        settle(steps[far - 1])
    settle(steps[far])
    gate_up(FIRST, NZ)
    loaded(19, 20)

    def down(lo, hi):
        def one(k):
            at = pl.ds(pl.multiple_of(k * WB, WB), WB)
            out = dot(hid[lo * MP : hi * MP], wd_v[:, at]).reshape(hi - lo, MP, WB)[:, :PC].astype(BF16)
            yp[0, lo:hi, k] = out[:, :, :LANES]
            yp[1, lo:hi, k] = out[:, :, LANES:]

        times(0, NE, one)

    def swap_y(g):
        lo, hi = ((FIRST, NZ), (0, FIRST))[g]
        part = pl.ds(lo, hi - lo)
        return remote(yp.at[1 - c, part], ysib.at[part], yss_sem.at[0], ysr_sem.at[g], sibling)

    down(FIRST, NZ)
    swap_y(0).start()

    def own(h, off):
        o = number[off % NZ]
        return yp[c, o, h * HE : (h + 1) * HE].astype(F32) + ysib[o, h * HE : (h + 1) * HE].astype(F32)

    def chain_right(h, s):
        return remote(yrs.at[h, s], yrr.at[h, s], ys_sem.at[0], yrr_sem.at[h, s], right)

    def chain_left(h, s):
        return remote(yls.at[h, s], ylr.at[h, s], ys_sem.at[0], ylr_sem.at[h, s], left)

    all_sent(ysib, yss_sem, ysr_sem)
    all_sent(ysib.at[pl.ds(0, NZ - 1)], ys_sem, yss_sem)

    def chain_step(s, lead):
        for h in pieces:
            if (h < NP // 2) == lead and s < hops_r[h]:
                part = own(h, hops_r[h] - s)
                if s > 0:
                    chain_right(h, s - 1).wait_recv()
                    part = part + yrr[h, s - 1].astype(F32)
                yrs[h, s] = part.astype(BF16)
                chain_right(h, s).start()
            if (h < NP // 2) != lead and s < hops_l[h]:
                part = own(h, s - hops_l[h])
                if s > 0:
                    chain_left(h, s - 1).wait_recv()
                    part = part + ylr[h, s - 1].astype(F32)
                yls[h, s] = part.astype(BF16)
                chain_left(h, s).start()

    swap_y(0).wait_recv()
    if FIRST <= NZ - 3:
        chain_step(0, True)
        down(0, FIRST)
        swap_y(1).start()
        chain_step(0, False)
        swap_y(1).wait_recv()
    else:
        down(0, FIRST)
        swap_y(1).start()
        swap_y(1).wait_recv()
        chain_step(0, True)
        chain_step(0, False)
    for s in range(1, far):
        chain_step(s, True)
        chain_step(s, False)

    def returned(k):
        return remote(ret_s.at[k], ret_r.at[e], rs_sem.at[0], rr_sem.at[0], (d, k))

    def give_back(k):
        @pl.when(e != k)
        def _():
            returned(k).start()

        @pl.when(e == k)
        def _():
            ret_r[k] = ret_s[k]

    all_sent(ret_s.at[pl.ds(0, NE - 1)], rs_sem, rr_sem)
    for h in pieces:
        part = own(h, 0)
        if hops_r[h] > 0:
            chain_right(h, hops_r[h] - 1).wait_recv()
            part = part + yrr[h, hops_r[h] - 1].astype(F32)
        if hops_l[h] > 0:
            chain_left(h, hops_l[h] - 1).wait_recv()
            part = part + ylr[h, hops_l[h] - 1].astype(F32)
        ret_s[h * HE : (h + 1) * HE] = part.astype(BF16)
        for k in range(h * HE, (h + 1) * HE):
            give_back(k)

    all_received(ret_r.at[pl.ds(0, NE - 1)], rs_sem, rr_sem)
    back_rows = ret_r[...].astype(F32).reshape(NE * PC, LANES).astype(BF16)
    final = stream_v[...].astype(F32) + dot(dhi_v[...], back_rows) + dot(dlo_v[...], back_rows)
    outg[c, z] = final.astype(BF16)

    def send_out(off):
        return remote(outg.at[c, z], outg.at[c, z], os_sem.at[0], or_sem.at[z], (2 * ((z + off) % NZ) + c, e))

    def wait_out(p):
        remote(outg.at[c, p], outg.at[c, p], os_sem.at[0], or_sem.at[p], (2 * z + c, e)).wait_recv()

    def pass_out(p):
        return remote(outg.at[c, p], outg.at[c, p], ts_sem.at[0], tr_sem.at[p], sibling)

    near = [off for k in range(far - 1, 0, -1) for off in (k, NZ - k)]
    for off in near:
        send_out(off).start()
    pass_out(z).start()
    all_sent(outg.at[0, pl.ds(0, len(near))], os_sem, or_sem)
    all_sent(outg.at[0], ts_sem, tr_sem)

    def half_way(p, side):
        part = outg.at[c, p, pl.ds(side * ROWS, ROWS)]
        return remote(part, part, fs_sem.at[0], fr_sem.at[side], (right, left)[side])

    for off in near:
        p = (z + off) % NZ
        wait_out(p)
        if off == NZ - (far - 1):
            half_way(p, 0).start()
        if off == far - 1:
            half_way(p, 1).start()
        pass_out(p).start()
    last = ahead_z(far)
    all_sent(outg.at[0, 0], fs_sem, fr_sem)
    for side in range(2):
        half_way(last, side).wait_recv()
    pass_out(last).start()

    def store_out(m, p):
        at = layer_out.at[pl.ds(pl.multiple_of(p * LW, LW), LW), pl.ds(pl.multiple_of(m * LANES, LANES), LANES)]
        return pltpu.make_async_copy(outg.at[m, p], at, out_sem.at[0])

    def wait_pass(p):
        remote(outg.at[1 - c, p], outg.at[1 - c, p], ts_sem.at[0], tr_sem.at[p], sibling).wait_recv()
        store_out(c, p).start()
        store_out(1 - c, p).start()

    for off in [0, *near, far]:
        wait_pass((z + off) % NZ)

    pltpu.make_async_copy(outg, outg, out_sem.at[0]).wait()

    for wait in ending:
        wait()


def hand_over(a, b, c, oa, ob, oc, va, vb, vc, sem):
    through = ((a, va, oa), (b, vb, ob), (c, vc, oc))
    first = [pltpu.make_async_copy(x, v, sem.at[i]) for i, (x, v, _) in enumerate(through)]
    second = [pltpu.make_async_copy(v, y, sem.at[i]) for i, (_, v, y) in enumerate(through)]
    for copy in first:
        copy.start()
    for one, two in zip(first, second):
        one.wait()
        two.start()
    for copy in second:
        copy.wait()


def body(
    ssm_state, conv_state, new_slot, conv_input, gate_input, conv_weight, conv_bias, x_proj_weight,
    step_weight, step_bias, decay_log, skip_gain, out_proj_weight, residual, norm_gain, routes,
    gate_weight, expert_gate, expert_up, expert_down,
):
    ROWS, NS, WB = ssm_state.shape
    NE = lax.axis_size("expert")
    NZ = lax.axis_size("dp") // 2
    RK = step_weight.shape[0]
    FB = expert_gate.shape[2]
    MC = 2 * ROWS // NE
    CAP = min(ROWS, 5 * ROWS * routes.shape[1] // (2 * NE))
    PC, LW, D, NP = 2 * CAP, 2 * ROWS, NE * WB, 4
    HE = NE // NP
    MP = (PC + 15) // 16 * 16
    RZ = ROWS // NZ
    far = NZ // 2
    hbm = pl.BlockSpec(memory_space=pl.ANY)
    V, S = pltpu.VMEM, pltpu.SemaphoreType.DMA
    scratch = [
        V((3, ROWS, WB), BF16), V((NZ, LW), jnp.int32), V((ROWS, WB), BF16), V((ROWS, WB), BF16),
        V((4, WB), F32), V((1, WB), F32), V((RK + 2 * NS, WB), BF16), V((RK, WB), BF16), V((1, WB), F32),
        V((NS, WB), F32), V((1, WB), F32), V((WB, WB), BF16), V((2 * NE, LANES), F32),
        V((2, LW), jnp.int32), V((2, LW), F32),
        V((ROWS, NS, WB), BF16), V((ROWS, NS, WB), F32), V((NS, ROWS, WB), F32), V((LW, LANES), BF16),
        V((FB, D), BF16), V((FB, D), BF16), V((FB, D), BF16),
        V((NE, 3, MC, WB), BF16), V((NE, 3, MC, WB), BF16),
        V((NE, NS, MC, WB), BF16), V((NE, NS, MC, WB), BF16),
        V((ROWS, NS, WB), BF16), V((3, ROWS, WB), BF16),
        V((NZ, RZ, RK + LANES), F32), V((2 * NZ, RZ, RK), F32), V((RZ, RK), F32), V((2, NZ, RZ, RK), F32),
        V((NE, ROWS, WB), BF16), V((2, NZ, LW, LANES), BF16), V((NZ, LW, LANES), BF16),
        V((NZ, LW, LANES), BF16), V((NZ, LW, LANES), BF16), V((LW, LANES), BF16),
        V((NE, PC, LANES), BF16), V((2, NZ, NE, PC, LANES), BF16), V((NZ, MP, D), BF16),
        V((NZ * MP, FB), F32), V((NZ * MP, FB), F32), V((NZ * MP, FB), BF16),
        V((2, NZ, NE, PC, LANES), BF16), V((NZ, NE, PC, LANES), BF16),
        V((NP, far, HE, PC, LANES), BF16), V((NP, far, HE, PC, LANES), BF16),
        V((NP, far, HE, PC, LANES), BF16), V((NP, far, HE, PC, LANES), BF16),
        V((NE, PC, LANES), BF16), V((NE, PC, LANES), BF16),
        V((NE * PC, LW), BF16), V((LW, NE * PC), BF16), V((LW, NE * PC), BF16), V((2, NZ, LW, LANES), BF16),
        S((20,)), S((1,)), S((1,)), S((1,)), S((1,)), S((2,)),
        S((1,)), S((1,)), S((1,)), S((1,)), S((1,)), S((NE,)),
        S((1,)), S((1,)), S((1,)), S((NZ,)), S((1,)), S((1,)),
        S((1,)), S((NP, far)), S((NP, far)), S((1,)), S((NZ,)),
        S((1,)), S((2,)), S((1,)), S((NP, far)), S((NP, far)),
        S((1,)), S((1,)), S((1,)), S((NZ,)), S((1,)), S((NZ,)), S((1,)), S((1,)), S((2,)),
    ]
    call = pl.pallas_call(
        functools.partial(kernel, (NE, NZ, ROWS, MC, CAP)),
        out_shape=(
            jax.ShapeDtypeStruct((ROWS, NS, WB), BF16),
            jax.ShapeDtypeStruct((3, ROWS, WB), BF16),
            jax.ShapeDtypeStruct((NE * ROWS, WB), BF16),
        ),
        in_specs=[hbm] * 20,
        out_specs=(hbm, hbm, hbm),
        scratch_shapes=scratch,
        compiler_params=pltpu.CompilerParams(
            collective_id=0, has_side_effects=True, vmem_limit_bytes=56 * 1024 * 1024
        ),
        name="decode_step",
    )
    ssm_new, conv_new, layer = call(
        ssm_state, conv_state.transpose(1, 0, 2), new_slot.reshape(NZ, LW), conv_input, gate_input,
        conv_weight, conv_bias.reshape(1, WB), x_proj_weight.T, step_weight, step_bias.reshape(1, WB),
        decay_log, skip_gain.reshape(1, WB), out_proj_weight, residual, norm_gain.reshape(2 * NE, LANES),
        routes.T, gate_weight.T, expert_gate[0].T, expert_up[0].T, expert_down[0],
    )
    shapes = [jax.ShapeDtypeStruct(v.shape, v.dtype) for v in (ssm_new, conv_new, layer)]
    ssm_new, conv_new, layer = pl.pallas_call(
        hand_over, out_shape=shapes, in_specs=[hbm] * 3, out_specs=[hbm] * 3, scratch_shapes=[*(V(v.shape, v.dtype) for v in shapes), S((3,))], name="hand_over"
    )(ssm_new, conv_new, layer)
    return ssm_new, conv_new.transpose(1, 0, 2), layer


def solution(mesh):
    in_specs = (
        P("expert", None, "dp"), P("expert", None, "dp"), P(), P("expert", "dp"), P("expert", "dp"),
        P(None, "dp"), P("dp"), P("dp", None), P(None, "dp"), P("dp"), P(None, "dp"), P("dp"),
        P("dp", "expert"), P(None, "expert"), P(), P(), P(),
        P("expert", None, "dp"), P("expert", None, "dp"), P("expert", "dp", None),
    )
    out_specs = (P("expert", None, "dp"), P("expert", None, "dp"), P(None, "expert"))
    return jax.shard_map(body, mesh=mesh, in_specs=in_specs, out_specs=out_specs, check_vma=False)
```

```python
import functools

import jax
import jax.numpy as jnp
from jax import lax
from jax.experimental import pallas as pl
from jax.experimental.pallas import tpu as pltpu
from jax.sharding import PartitionSpec as P

MESH = pl.DeviceIdType.MESH
F32 = jnp.float32
BF16 = jnp.bfloat16
LANES = 128


def iota(shape, axis):
    return lax.broadcasted_iota(jnp.int32, shape, axis)


def ones_where(mask):
    return jnp.where(mask, 1.0, 0.0)


def dot(a, b):
    return jnp.dot(a, b, preferred_element_type=F32)


def dot_t(a, b):
    return lax.dot_general(a, b, (((1,), (1,)), ((), ())), preferred_element_type=F32)


def silu(v):
    return v / (1.0 + jnp.exp(-v))


def times(lo, hi, step):
    def run(i, carry):
        step(i)
        return carry

    lax.fori_loop(lo, hi, run, 0)


def kernel(
    dims,
    ssm_hbm, conv_hbm, slot_hbm, cin_hbm, gin_hbm, cw_hbm, cb_hbm, xp_hbm, sw_hbm, sb_hbm,
    dl_hbm, sg_hbm, wo_hbm, res_hbm, ng_hbm, rt_hbm, gw_hbm, wg_hbm, wu_hbm, wd_hbm,
    ssm_out, conv_out, layer_out,
    conv_ref, slot_ref, cin_ref, gin_ref, cw_ref, cb_ref, xp_ref, sw_ref, sb_ref,
    dl_ref, sg_ref, wo_ref, ng_ref, rt_ref, gw_ref,
    ssm_v, ssm_f, moved_v, res_v, wg_v, wu_v, wd_v,
    conv_s, conv_r, ssm_s, ssm_r, ssm_o, conv_o,
    proj_s, proj_r, proj_c, proj_g,
    gat, mix_s, mix_b, mix_t, mix_r, stream_v,
    disp_s, xb, xn, acc_g, acc_u, hid, yp, ysib, yrs, yrr, yls, ylr,
    ret_s, ret_r, disp_v, dhi_v, dlo_v, outg,
    load_sem, cs_sem, cr_sem, ss_sem, sr_sem, store_sem,
    ps_sem, pr_sem, qs_sem, qr_sem, gs_sem, gr_sem,
    ms_sem, mr_sem, bs_sem, br_sem, ds_sem, dr_sem,
    xs_sem, xrr, xlr, xss, xsr,
    yss_sem, ysr_sem, ys_sem, yrr_sem, ylr_sem,
    rs_sem, rr_sem, os_sem, or_sem, ts_sem, tr_sem, out_sem, fs_sem, fr_sem,
):
    NE, NZ, ROWS, MC, CAP = dims
    ND = 2 * NZ
    PC = 2 * CAP
    LW = 2 * ROWS
    NS = dl_ref.shape[0]
    WB = cin_ref.shape[1]
    RK = sw_ref.shape[0]
    D = NE * WB
    NP = yrs.shape[0]
    HE = NE // NP
    MP = xn.shape[1]
    shift = ROWS.bit_length() - 1
    d = lax.axis_index("dp")
    e = lax.axis_index("expert")
    z = d // 2
    c = d % 2

    def remote(src, dst, ssem, rsem, dev):
        return pltpu.make_async_remote_copy(
            src_ref=src, dst_ref=dst, send_sem=ssem, recv_sem=rsem, device_id=dev, device_id_type=MESH
        )

    ending = []

    barrier = pltpu.get_barrier_semaphore()
    for i in range(1, ND):
        pl.semaphore_signal(barrier, inc=1, device_id=((d + i) % ND, e), device_id_type=MESH)
    for i in range(1, NE):
        pl.semaphore_signal(barrier, inc=1, device_id=(d, (e + i) % NE), device_id_type=MESH)

    row0 = pl.multiple_of(z * LW, LW)
    lane0 = pl.multiple_of(c * LANES, LANES)
    pair = pl.ds(row0, LW)
    sources = [
        (conv_hbm, conv_ref), (slot_hbm, slot_ref), (ssm_hbm, ssm_v), (rt_hbm.at[:, pair], rt_ref),
        (gw_hbm.at[:, pair], gw_ref), (cin_hbm, cin_ref), (cw_hbm, cw_ref), (cb_hbm, cb_ref), (xp_hbm, xp_ref),
        (sw_hbm, sw_ref), (sb_hbm, sb_ref), (dl_hbm, dl_ref), (sg_hbm, sg_ref), (gin_hbm, gin_ref), (wo_hbm, wo_ref),
        (res_hbm.at[pair, pl.ds(lane0, LANES)], res_v), (ng_hbm, ng_ref), (wg_hbm, wg_v), (wu_hbm, wu_v), (wd_hbm, wd_v),
    ]
    loads = [pltpu.make_async_copy(src, dst, load_sem.at[i]) for i, (src, dst) in enumerate(sources)]
    for load in loads:
        load.start()

    def loaded(lo, hi):
        for load in loads[lo:hi]:
            load.wait()

    loaded(0, 2)

    mine = slot_ref[pl.ds(e // 2, 1), :]
    mine = jnp.where(e % 2 == 0, mine[:, :ROWS], mine[:, ROWS:])
    target = lax.shift_right_logical(mine, shift)
    target_hot = ones_where(iota((NE, ROWS), 0) == target)
    before = ones_where(iota((ROWS, ROWS), 0) < iota((ROWS, ROWS), 1)).astype(BF16)
    ahead = dot(target_hot.astype(BF16), before)
    earlier = jnp.sum(target_hot * ahead, axis=0, keepdims=True).astype(jnp.int32)
    pack = ones_where(iota((NE * MC, ROWS), 0) == target * MC + earlier).astype(BF16)
    for k in range(3):
        conv_s[:, k] = dot(pack, conv_ref[k]).reshape(NE, MC, WB).astype(BF16)

    loaded(2, 3)
    ssm_f[...] = ssm_v[...].astype(F32)
    for n in range(NS):
        ssm_s[:, n] = dot(pack, ssm_f[:, n, :].astype(BF16)).reshape(NE, MC, WB).astype(BF16)

    slots = slot_ref[...]
    arriving = ones_where(lax.shift_right_logical(slots, shift) == e)
    lane = iota((LW, LW), 1)
    sub = iota((LW, LW), 0)
    before2 = ones_where((sub < lane) & ((sub < ROWS) == (lane < ROWS))).astype(BF16)
    rank = dot(arriving.astype(BF16), before2)
    place = (slots & (ROWS - 1)).astype(F32) + 1.0
    half = iota((NZ, LW), 1) >= ROWS
    to_lane = iota((NZ, NE * MC), 1) - iota((NZ, NE * MC), 0) * (2 * MC)
    spread = jnp.zeros((NZ, NE * MC), F32)
    for h in range(2):
        live = (arriving > 0.0) & (half == bool(h))
        for k in range(MC):
            found = jnp.sum(jnp.where(live & (rank == float(k)), place, 0.0), axis=1, keepdims=True)
            spread = spread + jnp.where(to_lane == h * MC + k, found, 0.0)
    row_of = jnp.sum(spread, axis=0, keepdims=True).astype(jnp.int32) - 1
    unpack = ones_where(iota((ROWS, NE * MC), 0) == row_of).astype(BF16)

    loaded(3, 5)
    r0 = rt_ref[0:1, :]
    r1 = rt_ref[1:2, :]
    g0 = gw_ref[0:1, :]
    g1 = gw_ref[1:2, :]
    expert_id = iota((NE, LW), 0)
    named = ones_where((expert_id == r0) | (expert_id == r1))
    weight = jnp.where(expert_id == r0, g0, 0.0) + jnp.where(expert_id == r1, g1, 0.0)
    w_hi = weight.astype(BF16).astype(F32)
    w_lo = weight - w_hi
    in_block = dot(named.astype(BF16), before2).astype(jnp.int32)
    seat = in_block + jnp.where(iota((NE, LW), 1) >= ROWS, CAP, 0)
    seat = jnp.where(named > 0.0, seat, -1)
    seat_id = iota((PC, LW), 0)
    rows_d, rows_hi, rows_lo = [], [], []
    for k in range(NE):
        hit = seat_id == seat[k : k + 1, :]
        rows_d.append(jnp.where(hit, 1.0, 0.0))
        rows_hi.append(jnp.where(hit, w_hi[k : k + 1, :], 0.0))
        rows_lo.append(jnp.where(hit, w_lo[k : k + 1, :], 0.0))
    disp_v[...] = jnp.concatenate(rows_d, axis=0).astype(BF16)
    dhi_v[...] = jnp.concatenate(rows_hi, axis=0).T.astype(BF16)
    dlo_v[...] = jnp.concatenate(rows_lo, axis=0).T.astype(BF16)

    def all_sent(some, ssem, rsem):
        ending.append(remote(some, some, ssem.at[0], rsem.at[0], (d, e)).wait_send)

    def all_received(some, ssem, rsem):
        remote(some, some, ssem.at[0], rsem.at[0], (d, e)).wait_recv()

    def to_experts(src_of, dst, some, ssem, rsem):
        for i in range(1, NE):
            p = (e + i) % NE
            remote(src_of(p), dst, ssem.at[0], rsem.at[0], (d, p)).start()
        all_sent(some, ssem, rsem)

    pl.semaphore_wait(barrier, NE - 1 + ND - 1)

    to_experts(lambda p: conv_s.at[p], conv_r.at[e], conv_s.at[pl.ds(0, NE - 1)], cs_sem, cr_sem)
    conv_r[e] = conv_s[e]
    ssm_r[e] = ssm_s[e]

    loaded(5, 9)
    all_received(conv_r.at[pl.ds(0, NE - 1)], cs_sem, cr_sem)
    to_experts(lambda p: ssm_s.at[p], ssm_r.at[e], ssm_s.at[pl.ds(0, NE - 1)], ss_sem, sr_sem)
    window = []
    for k in range(3):
        got = conv_r[:, k].astype(F32).reshape(NE * MC, WB).astype(BF16)
        window.append(dot(unpack, got))
    conv_o[0] = window[1].astype(BF16)
    conv_o[1] = window[2].astype(BF16)
    conv_o[2] = cin_ref[...]
    window.append(cin_ref[...].astype(F32))
    total = window[0] * cw_ref[0:1, :]
    for k in range(1, 4):
        total = total + window[k] * cw_ref[k : k + 1, :]
    activated = silu(total + cb_ref[...]).astype(BF16)
    act = activated.astype(F32)
    partial = dot_t(activated, xp_ref[...])
    RZ = ROWS // NZ
    proj_s[...] = jnp.zeros_like(proj_s)
    proj_s[:, :, : RK + 2 * NS] = partial.reshape(NZ, RZ, RK + 2 * NS)

    def proj_src(p):
        return proj_s.at[p // 2, :, pl.ds(pl.multiple_of((p % 2) * LANES, LANES), RK)]

    def to_dp(src_of, dst, some, ssem, rsem):
        for i in range(1, ND):
            p = (d + i) % ND
            remote(src_of(p), dst, ssem.at[0], rsem.at[0], (p, e)).start()
        all_sent(some, ssem, rsem)

    others = pl.ds(0, ND - 1)
    to_dp(proj_src, proj_r.at[d], proj_r.at[others], ps_sem, pr_sem)
    proj_r[d] = proj_s[z, :, pl.ds(lane0, RK)]
    store_conv = pltpu.make_async_copy(conv_o, conv_out, store_sem.at[0])
    store_conv.start()
    ending.append(store_conv.wait)

    all_received(proj_r.at[others], ps_sem, pr_sem)
    summed = proj_r[0]
    for k in range(1, ND):
        summed = summed + proj_r[k]
    proj_c[...] = summed
    to_dp(lambda p: proj_c, proj_g.at[c, z], proj_r.at[others], qs_sem, qr_sem)
    proj_g[c, z] = summed
    all_received(ssm_r.at[pl.ds(0, NE - 1)], ss_sem, sr_sem)
    for n in range(NS):
        got = ssm_r[:, n].astype(F32).reshape(NE * MC, WB).astype(BF16)
        moved_v[n] = dot(unpack, got)
    loaded(9, 14)
    gate = silu(gin_ref[...].astype(F32))
    decay = -jnp.exp(dl_ref[...])
    all_received(proj_r.at[others], qs_sem, qr_sem)
    step_low = proj_g[0].reshape(ROWS, RK)
    coef = proj_g[1][:, :, RK - LANES :].reshape(ROWS, LANES)
    mean = jnp.sum(step_low * step_low, axis=1, keepdims=True) * (1.0 / RK)
    step_norm = (step_low * lax.rsqrt(mean + 1e-06)).astype(BF16)
    pre = dot(step_norm, sw_ref[...]) + sb_ref[...]
    step = jnp.maximum(pre, 0.0) + jnp.log1p(jnp.exp(-jnp.abs(pre)))
    push = step * act

    y = sg_ref[...] * act
    read = jnp.zeros_like(y)
    for n in range(NS):
        state = jnp.exp(step * decay[n : n + 1, :]) * moved_v[n] + push * coef[:, n : n + 1]
        ssm_f[:, n, :] = state
        read = read + coef[:, NS + n : NS + n + 1] * state
    gated = ((read + y) * gate).astype(BF16)
    gat[e] = gated
    for i in range(1, NE):
        remote(gat.at[e], gat.at[e], gs_sem.at[0], gr_sem.at[e], (d, (e + i) % NE)).start()
    all_sent(gat.at[pl.ds(0, NE - 1)], gs_sem, gr_sem)
    ssm_o[...] = ssm_f[...].astype(BF16)
    store_ssm = pltpu.make_async_copy(ssm_o, ssm_out, store_sem.at[1])
    store_ssm.start()
    ending.append(store_ssm.wait)

    loaded(14, 16)
    sibling = (2 * z + 1 - c, e)

    def swap_mix(p):
        return remote(mix_s.at[1 - c, p], mix_b.at[p], bs_sem.at[0], br_sem.at[p], sibling)

    def arrived(p):
        @pl.when(p != e)
        def _():
            remote(gat.at[p], gat.at[p], gs_sem.at[0], gr_sem.at[p], (d, p)).wait_recv()

    def project(p):
        arrived(2 * p)
        arrived(2 * p + 1)
        mixed = dot(gat[pl.ds(2 * p, 2)].reshape(LW, WB), wo_ref[...])
        mix_s[0, p] = mixed[:, :LANES].astype(BF16)
        mix_s[1, p] = mixed[:, LANES:].astype(BF16)
        swap_mix(p).start()

    def send_mix(i):
        p = (z + i) % NZ
        return remote(mix_t.at[p], mix_r.at[z], ms_sem.at[0], mr_sem.at[0], (2 * p + c, e))

    def join(i):
        p = (z + i) % NZ
        swap_mix(p).wait_recv()
        mix_t[p] = (mix_s[c, p].astype(F32) + mix_b[p].astype(F32)).astype(BF16)
        if i > 0:
            send_mix(i).start()

    all_sent(mix_b, bs_sem, br_sem)
    order = [*range(1, NZ), 0]
    for at, i in enumerate(order):
        project((z + i) % NZ)
        if at > 0:
            join(order[at - 1])
    join(0)
    mix_r[z] = mix_t[z]
    all_sent(mix_t.at[pl.ds(0, NZ - 1)], ms_sem, mr_sem)

    all_received(mix_r.at[pl.ds(0, NZ - 1)], ms_sem, mr_sem)
    mixed = mix_r[0].astype(F32)
    for k in range(1, NZ):
        mixed = mixed + mix_r[k].astype(F32)
    stream = (res_v[...].astype(F32) + mixed).astype(BF16)
    stream_v[...] = stream

    disp_s[...] = dot(disp_v[...], stream).reshape(NE, PC, LANES).astype(BF16)
    to_experts(lambda p: disp_s.at[p], xb.at[c, z, e], disp_s.at[pl.ds(0, NE - 1)], ds_sem, dr_sem)
    xb[c, z, e] = disp_s[e]
    all_received(disp_s.at[pl.ds(0, NE - 1)], ds_sem, dr_sem)

    right = (2 * ((z + 1) % NZ) + c, e)
    left = (2 * ((z + NZ - 1) % NZ) + c, e)
    far = NZ // 2
    pieces = range(NP)
    hops_r = [far if h < NP // 2 else NZ - 1 - far for h in pieces]
    hops_l = [NZ - 1 - far if h < NP // 2 else far for h in pieces]
    halves = [pl.ds(h * HE, HE) for h in pieces]

    def back(s):
        return (z + NZ - s) % NZ

    def ahead_z(s):
        return (z + s) % NZ

    def ring_right(h, s):
        p = back(s)
        part = xb.at[c, p, halves[h]]
        return remote(part, part, xs_sem.at[0], xrr.at[h, s], right)

    def ring_left(h, s):
        p = ahead_z(s)
        part = xb.at[c, p, halves[h]]
        return remote(part, part, xs_sem.at[0], xlr.at[h, s], left)

    def wait_right(h, s):
        part = xb.at[c, back(s + 1), halves[h]]
        remote(part, part, xs_sem.at[0], xrr.at[h, s], right).wait_recv()

    def wait_left(h, s):
        part = xb.at[c, ahead_z(s + 1), halves[h]]
        remote(part, part, xs_sem.at[0], xlr.at[h, s], left).wait_recv()

    def over(p):
        return remote(xb.at[c, p], xb.at[c, p], xss.at[0], xsr.at[p], sibling)

    def wait_over(p):
        remote(xb.at[1 - c, p], xb.at[1 - c, p], xss.at[0], xsr.at[p], sibling).wait_recv()

    all_sent(xb.at[0], xss, xsr)
    all_sent(xb.at[0, pl.ds(0, NZ - 1)], xs_sem, xss)

    def normalise(o, p):
        square = jnp.zeros((PC, LANES), F32)
        for k in range(NE):
            for m in range(2):
                v = xb[m, p, k].astype(F32)
                square = square + v * v
        scale = lax.rsqrt(jnp.sum(square, axis=1, keepdims=True) * (1.0 / D) + 1e-05)
        for k in range(NE):
            for m in range(2):
                v = xb[m, p, k].astype(F32) * scale * ng_ref[2 * k + m : 2 * k + m + 1, :]
                if MP > PC:
                    v = jnp.concatenate([v, jnp.zeros((MP - PC, LANES), F32)], axis=0)
                xn[o, :, (2 * k + m) * LANES : (2 * k + m + 1) * LANES] = v.astype(BF16)

    steps = [[(0, z, 0)]]
    for s in range(1, far):
        steps.append([(2 * s - 1, back(s), -s), (2 * s, ahead_z(s), s)])
    steps.append([(NZ - 1, ahead_z(far), far)])
    number = {off % NZ: o for group in steps for o, _, off in group}
    FIRST = sum(len(group) for group in steps[: max(1, far - 1)])
    KC = min(D, 2048)

    def gate_up(lo, hi):
        rows = pl.ds(lo * MP, (hi - lo) * MP)
        acc_g[rows] = jnp.zeros(((hi - lo) * MP, acc_g.shape[1]), F32)
        acc_u[rows] = jnp.zeros(((hi - lo) * MP, acc_u.shape[1]), F32)

        def depth(k):
            at = pl.ds(pl.multiple_of(k * KC, KC), KC)
            x = xn[lo:hi, :, at].reshape((hi - lo) * MP, KC)
            acc_g[rows] += dot_t(x, wg_v[:, at])
            acc_u[rows] += dot_t(x, wu_v[:, at])

        times(0, D // KC, depth)
        hid[rows] = (silu(acc_g[rows]) * acc_u[rows]).astype(BF16)

    def settle(group):
        for o, p, _ in group:
            wait_over(p)
            normalise(o, p)

    loaded(16, 19)
    def ring_step(s, lead):
        for h in pieces:
            if (h < NP // 2) == lead:
                if 0 < s <= hops_r[h]:
                    wait_right(h, s - 1)
                if s < hops_r[h]:
                    ring_right(h, s).start()
            else:
                if 0 < s <= hops_l[h]:
                    wait_left(h, s - 1)
                if s < hops_l[h]:
                    ring_left(h, s).start()

    for s in range(far + 1):
        ring_step(s, True)
        if s == 0:
            over(z).start()
            settle(steps[0])
        ring_step(s, False)
        if s > 0:
            for _, p, _ in steps[s]:
                over(p).start()
        if 0 < s < far - 1:
            settle(steps[s])
        if s == max(1, far - 1):
            gate_up(0, FIRST)
    if far > 1:
        settle(steps[far - 1])
    settle(steps[far])
    gate_up(FIRST, NZ)
    loaded(19, 20)

    def down(lo, hi):
        def one(k):
            at = pl.ds(pl.multiple_of(k * WB, WB), WB)
            out = dot(hid[lo * MP : hi * MP], wd_v[:, at]).reshape(hi - lo, MP, WB)[:, :PC].astype(BF16)
            yp[0, lo:hi, k] = out[:, :, :LANES]
            yp[1, lo:hi, k] = out[:, :, LANES:]

        times(0, NE, one)

    def swap_y(g):
        lo, hi = ((FIRST, NZ), (0, FIRST))[g]
        part = pl.ds(lo, hi - lo)
        return remote(yp.at[1 - c, part], ysib.at[part], yss_sem.at[0], ysr_sem.at[g], sibling)

    down(FIRST, NZ)
    swap_y(0).start()

    def own(h, off):
        o = number[off % NZ]
        return yp[c, o, h * HE : (h + 1) * HE].astype(F32) + ysib[o, h * HE : (h + 1) * HE].astype(F32)

    def chain_right(h, s):
        return remote(yrs.at[h, s], yrr.at[h, s], ys_sem.at[0], yrr_sem.at[h, s], right)

    def chain_left(h, s):
        return remote(yls.at[h, s], ylr.at[h, s], ys_sem.at[0], ylr_sem.at[h, s], left)

    all_sent(ysib, yss_sem, ysr_sem)
    all_sent(ysib.at[pl.ds(0, NZ - 1)], ys_sem, yss_sem)

    def chain_step(s, lead):
        for h in pieces:
            if (h < NP // 2) == lead and s < hops_r[h]:
                part = own(h, hops_r[h] - s)
                if s > 0:
                    chain_right(h, s - 1).wait_recv()
                    part = part + yrr[h, s - 1].astype(F32)
                yrs[h, s] = part.astype(BF16)
                chain_right(h, s).start()
            if (h < NP // 2) != lead and s < hops_l[h]:
                part = own(h, s - hops_l[h])
                if s > 0:
                    chain_left(h, s - 1).wait_recv()
                    part = part + ylr[h, s - 1].astype(F32)
                yls[h, s] = part.astype(BF16)
                chain_left(h, s).start()

    swap_y(0).wait_recv()
    if FIRST <= NZ - 3:
        chain_step(0, True)
        down(0, FIRST)
        swap_y(1).start()
        chain_step(0, False)
        swap_y(1).wait_recv()
    else:
        down(0, FIRST)
        swap_y(1).start()
        swap_y(1).wait_recv()
        chain_step(0, True)
        chain_step(0, False)
    for s in range(1, far):
        chain_step(s, True)
        chain_step(s, False)

    def returned(k):
        return remote(ret_s.at[k], ret_r.at[e], rs_sem.at[0], rr_sem.at[0], (d, k))

    def give_back(k):
        @pl.when(e != k)
        def _():
            returned(k).start()

        @pl.when(e == k)
        def _():
            ret_r[k] = ret_s[k]

    all_sent(ret_s.at[pl.ds(0, NE - 1)], rs_sem, rr_sem)
    for h in pieces:
        part = own(h, 0)
        if hops_r[h] > 0:
            chain_right(h, hops_r[h] - 1).wait_recv()
            part = part + yrr[h, hops_r[h] - 1].astype(F32)
        if hops_l[h] > 0:
            chain_left(h, hops_l[h] - 1).wait_recv()
            part = part + ylr[h, hops_l[h] - 1].astype(F32)
        ret_s[h * HE : (h + 1) * HE] = part.astype(BF16)
        for k in range(h * HE, (h + 1) * HE):
            give_back(k)

    all_received(ret_r.at[pl.ds(0, NE - 1)], rs_sem, rr_sem)
    back_rows = ret_r[...].astype(F32).reshape(NE * PC, LANES).astype(BF16)
    final = stream_v[...].astype(F32) + dot(dhi_v[...], back_rows) + dot(dlo_v[...], back_rows)
    outg[c, z] = final.astype(BF16)

    def send_out(off):
        return remote(outg.at[c, z], outg.at[c, z], os_sem.at[0], or_sem.at[z], (2 * ((z + off) % NZ) + c, e))

    def wait_out(p):
        remote(outg.at[c, p], outg.at[c, p], os_sem.at[0], or_sem.at[p], (2 * z + c, e)).wait_recv()

    def pass_out(p):
        return remote(outg.at[c, p], outg.at[c, p], ts_sem.at[0], tr_sem.at[p], sibling)

    near = [off for k in range(far - 1, 0, -1) for off in (k, NZ - k)]
    for off in near:
        send_out(off).start()
    pass_out(z).start()
    all_sent(outg.at[0, pl.ds(0, len(near))], os_sem, or_sem)
    all_sent(outg.at[0], ts_sem, tr_sem)

    def half_way(p, side):
        part = outg.at[c, p, pl.ds(side * ROWS, ROWS)]
        return remote(part, part, fs_sem.at[0], fr_sem.at[side], (right, left)[side])

    for off in near:
        p = (z + off) % NZ
        wait_out(p)
        if off == NZ - (far - 1):
            half_way(p, 0).start()
        if off == far - 1:
            half_way(p, 1).start()
        pass_out(p).start()
    last = ahead_z(far)
    all_sent(outg.at[0, 0], fs_sem, fr_sem)
    for side in range(2):
        half_way(last, side).wait_recv()
    pass_out(last).start()

    def store_out(m, p):
        at = layer_out.at[pl.ds(pl.multiple_of(p * LW, LW), LW), pl.ds(pl.multiple_of(m * LANES, LANES), LANES)]
        return pltpu.make_async_copy(outg.at[m, p], at, out_sem.at[0])

    def wait_pass(p):
        remote(outg.at[1 - c, p], outg.at[1 - c, p], ts_sem.at[0], tr_sem.at[p], sibling).wait_recv()
        store_out(c, p).start()
        store_out(1 - c, p).start()

    for off in [0, *near, far]:
        wait_pass((z + off) % NZ)

    pltpu.make_async_copy(outg, outg, out_sem.at[0]).wait()

    for wait in ending:
        wait()


def hand_over(a, b, c, oa, ob, oc, va, vb, vc, sem):
    through = ((a, va, oa), (b, vb, ob), (c, vc, oc))
    first = [pltpu.make_async_copy(x, v, sem.at[i]) for i, (x, v, _) in enumerate(through)]
    second = [pltpu.make_async_copy(v, y, sem.at[i]) for i, (_, v, y) in enumerate(through)]
    for copy in first:
        copy.start()
    for one, two in zip(first, second):
        one.wait()
        two.start()
    for copy in second:
        copy.wait()


def body(
    ssm_state, conv_state, new_slot, conv_input, gate_input, conv_weight, conv_bias, x_proj_weight,
    step_weight, step_bias, decay_log, skip_gain, out_proj_weight, residual, norm_gain, routes,
    gate_weight, expert_gate, expert_up, expert_down,
):
    ROWS, NS, WB = ssm_state.shape
    NE = lax.axis_size("expert")
    NZ = lax.axis_size("dp") // 2
    RK = step_weight.shape[0]
    FB = expert_gate.shape[2]
    MC = 2 * ROWS // NE
    CAP = min(ROWS, 5 * ROWS * routes.shape[1] // (2 * NE))
    PC, LW, D, NP = 2 * CAP, 2 * ROWS, NE * WB, 4
    HE = NE // NP
    MP = (PC + 15) // 16 * 16
    RZ = ROWS // NZ
    far = NZ // 2
    hbm = pl.BlockSpec(memory_space=pl.ANY)
    V, S = pltpu.VMEM, pltpu.SemaphoreType.DMA
    scratch = [
        V((3, ROWS, WB), BF16), V((NZ, LW), jnp.int32), V((ROWS, WB), BF16), V((ROWS, WB), BF16),
        V((4, WB), F32), V((1, WB), F32), V((RK + 2 * NS, WB), BF16), V((RK, WB), BF16), V((1, WB), F32),
        V((NS, WB), F32), V((1, WB), F32), V((WB, WB), BF16), V((2 * NE, LANES), F32),
        V((2, LW), jnp.int32), V((2, LW), F32),
        V((ROWS, NS, WB), BF16), V((ROWS, NS, WB), F32), V((NS, ROWS, WB), F32), V((LW, LANES), BF16),
        V((FB, D), BF16), V((FB, D), BF16), V((FB, D), BF16),
        V((NE, 3, MC, WB), BF16), V((NE, 3, MC, WB), BF16),
        V((NE, NS, MC, WB), BF16), V((NE, NS, MC, WB), BF16),
        V((ROWS, NS, WB), BF16), V((3, ROWS, WB), BF16),
        V((NZ, RZ, RK + LANES), F32), V((2 * NZ, RZ, RK), F32), V((RZ, RK), F32), V((2, NZ, RZ, RK), F32),
        V((NE, ROWS, WB), BF16), V((2, NZ, LW, LANES), BF16), V((NZ, LW, LANES), BF16),
        V((NZ, LW, LANES), BF16), V((NZ, LW, LANES), BF16), V((LW, LANES), BF16),
        V((NE, PC, LANES), BF16), V((2, NZ, NE, PC, LANES), BF16), V((NZ, MP, D), BF16),
        V((NZ * MP, FB), F32), V((NZ * MP, FB), F32), V((NZ * MP, FB), BF16),
        V((2, NZ, NE, PC, LANES), BF16), V((NZ, NE, PC, LANES), BF16),
        V((NP, far, HE, PC, LANES), BF16), V((NP, far, HE, PC, LANES), BF16),
        V((NP, far, HE, PC, LANES), BF16), V((NP, far, HE, PC, LANES), BF16),
        V((NE, PC, LANES), BF16), V((NE, PC, LANES), BF16),
        V((NE * PC, LW), BF16), V((LW, NE * PC), BF16), V((LW, NE * PC), BF16), V((2, NZ, LW, LANES), BF16),
        S((20,)), S((1,)), S((1,)), S((1,)), S((1,)), S((2,)),
        S((1,)), S((1,)), S((1,)), S((1,)), S((1,)), S((NE,)),
        S((1,)), S((1,)), S((1,)), S((NZ,)), S((1,)), S((1,)),
        S((1,)), S((NP, far)), S((NP, far)), S((1,)), S((NZ,)),
        S((1,)), S((2,)), S((1,)), S((NP, far)), S((NP, far)),
        S((1,)), S((1,)), S((1,)), S((NZ,)), S((1,)), S((NZ,)), S((1,)), S((1,)), S((2,)),
    ]
    call = pl.pallas_call(
        functools.partial(kernel, (NE, NZ, ROWS, MC, CAP)),
        out_shape=(
            jax.ShapeDtypeStruct((ROWS, NS, WB), BF16),
            jax.ShapeDtypeStruct((3, ROWS, WB), BF16),
            jax.ShapeDtypeStruct((NE * ROWS, WB), BF16),
        ),
        in_specs=[hbm] * 20,
        out_specs=(hbm, hbm, hbm),
        scratch_shapes=scratch,
        compiler_params=pltpu.CompilerParams(
            collective_id=0, has_side_effects=True, vmem_limit_bytes=56 * 1024 * 1024
        ),
        name="decode_step",
    )
    ssm_new, conv_new, layer = call(
        ssm_state, conv_state.transpose(1, 0, 2), new_slot.reshape(NZ, LW), conv_input, gate_input,
        conv_weight, conv_bias.reshape(1, WB), x_proj_weight.T, step_weight, step_bias.reshape(1, WB),
        decay_log, skip_gain.reshape(1, WB), out_proj_weight, residual, norm_gain.reshape(2 * NE, LANES),
        routes.T, gate_weight.T, expert_gate[0].T, expert_up[0].T, expert_down[0],
    )
    shapes = [jax.ShapeDtypeStruct(v.shape, v.dtype) for v in (ssm_new, conv_new, layer)]
    ssm_new, conv_new, layer = pl.pallas_call(
        hand_over, out_shape=shapes, in_specs=[hbm] * 3, out_specs=[hbm] * 3, scratch_shapes=[*(V(v.shape, v.dtype) for v in shapes), S((3,))], name="hand_over"
    )(ssm_new, conv_new, layer)
    return ssm_new, conv_new.transpose(1, 0, 2), layer


def solution(mesh):
    in_specs = (
        P("expert", None, "dp"), P("expert", None, "dp"), P(), P("expert", "dp"), P("expert", "dp"),
        P(None, "dp"), P("dp"), P("dp", None), P(None, "dp"), P("dp"), P(None, "dp"), P("dp"),
        P("dp", "expert"), P(None, "expert"), P(), P(), P(),
        P("expert", None, "dp"), P("expert", None, "dp"), P("expert", "dp", None),
    )
    out_specs = (P("expert", None, "dp"), P("expert", None, "dp"), P(None, "expert"))
    return jax.shard_map(body, mesh=mesh, in_specs=in_specs, out_specs=out_specs, check_vma=False)
```
